256 devices in a mesh: frame: 16 (over x, z_lo), fsdp: 16 (over z_hi, y, core).
Axes of the slice: x: 4, y: 4, z: 8 (z_hi: 2, z_lo: 4; z = z_hi * 4 + z_lo), core: 2. Of those that a mesh axis runs over, the one named last changes fastest.
Arguments:
- queries: bfloat16 [256, 192, 3072], P(('frame', 'fsdp')), may hold values from -18 to 18
- keys: bfloat16 [256, 192, 3072], P(('frame', 'fsdp')), may hold values from -7 to 7
- values: bfloat16 [256, 192, 3072], P(('frame', 'fsdp')), may hold values from -6 to 6
- residual: bfloat16 [256, 192, 3072], P(('frame', 'fsdp')), may hold values from -6 to 6
- target: bfloat16 [256, 192, 3072], P(('frame', 'fsdp')), may hold values from -6 to 6
- output_weight: bfloat16 [3072, 3072], P('fsdp'), may hold values from -0.109375 to 0.109375
- down_adapter: bfloat16 [16, 64, 3072], P('frame', None, 'fsdp'), may hold values from -0.109375 to 0.109375
- up_adapter: bfloat16 [16, 64, 3072], P('frame', None, 'fsdp'), may hold values from -1.1953125 to 1.1953125
- scene_of_frame: int32 [256], P(('frame', 'fsdp')), may hold values from 0 to 15
- scene_adapter_row: int32 [16], replicated, may hold values from 0 to 15, each once
- valid_token_count: int32 [256], P(('frame', 'fsdp')), may hold values from 1 to 192, 30720 in all
Outputs:
- grad_down: float32 [16, 64, 3072], P('frame', None, 'fsdp')
- grad_up: float32 [16, 64, 3072], P('frame', None, 'fsdp')
- frame_loss: float32 [256], P(('frame', 'fsdp'))
The draws below stay inside these ranges and needn't reach their ends.
Inputs may be any that keep to these rules, and one draw needn't show every extreme that they name: `scene_adapter_row`: each scene has its own adapter row. `valid_token_count`: some frame has all 192 slots valid.
All inputs are finite; a program needn't handle non-finite values. No bound on the sum of `valid_token_count` on one device may be relied on, other than what follows from the above.
Results may differ from the reference program's by a relative error of at most 0.0053.
Values may be sent and summed in bfloat16 or wider, within the bound.
A program may use at most 192 MiB of HBM per device.

```python
import math
import jax
import jax.numpy as jnp
import numpy as np
from jax import lax

MODEL_DIM = 3072
HEADS = 24
HD = 128
ADAPTER_RANK = 64
FT = 192
FRAMES = 256
SCENE_COUNT = 16


def key_field(key):
    field_base = jnp.clip(jax.random.normal(jax.random.fold_in(key, 31), (FRAMES, FT, MODEL_DIM), jnp.float32), -6.0, 6.0)
    return field_base


def draw_keys(key, part):
    return key_field(key).astype(jnp.bfloat16)


def draw_queries(key, part):
    query_base = jnp.clip(jax.random.normal(jax.random.fold_in(key, 41), (FRAMES, FT, MODEL_DIM), jnp.float32), -6.0, 6.0)
    return query_base.astype(jnp.bfloat16)


def with_ends(values, rng, smallest, top_value):
    longest = values.shape.index(max(values.shape))
    spots = []
    for shift in (0, 1):
        where = [jax.random.randint(jax.random.fold_in(rng, axis), (), 0, length) for axis, length in enumerate(values.shape)]
        where[longest] = (where[longest] + shift) % values.shape[longest]
        spots.append(tuple(where))
    return values.at[spots[0]].set(smallest).at[spots[1]].set(top_value)


def steps_of(rng, shape, cuts, least, largest):
    def one(axis_at, blocks):
        steps = jax.random.uniform(jax.random.fold_in(jax.random.fold_in(rng, 6), axis_at), (blocks,), jnp.float32, least / len(cuts), largest / len(cuts))
        return jnp.repeat(jnp.exp(steps), shape[axis_at] // blocks).reshape((-1,) + (1,) * (len(shape) - axis_at - 1))

    level = one(*cuts[0])
    for cut in cuts[1:]:
        level = level * one(*cut)
    return level


def rank_table(count, skew):
    portions = [(1 << 20) // math.isqrt(rank ** skew) + 1 for rank in range(1, count + 1)]
    deviation = 1 + sum(portions) // (1 << 30)
    return np.cumsum(np.array([max(1, weight // deviation) for weight in portions]))


def ranked(own_key, dims, amount, lean):
    grid = rank_table(amount, lean)
    ticket = jax.random.randint(jax.random.fold_in(own_key, 1), dims, 0, int(grid[amount - 1]))
    grade = jnp.searchsorted(jnp.asarray(grid, jnp.int32), ticket, side="right")
    return jax.random.permutation(jax.random.fold_in(own_key, 2), amount)[grade].astype(jnp.int32)


def length_profile(count, total, limit, skew):
    weights = [(1 << 20) // math.isqrt(grade ** skew) + 1 for grade in range(2, count + 1)]
    rest, counts = total - limit - (count - 1), [1] * (count - 1)
    while rest > 0:
        movable = [i for i in range(count - 1) if counts[i] < limit]
        mass, left = sum([weights[i] for i in movable]), rest
        for i in movable:
            addition = min(limit - counts[i], max(1, left * weights[i] // mass), rest)
            counts[i] = counts[i] + addition
            rest = rest - addition
    return np.array([limit] + counts)


def ragged(stream_key, count, total, bound, skew):
    if count == 2:
        one = jax.random.randint(stream_key, (), max(1, total - bound), min(bound, total - 1) + 1)
        return jnp.stack([one, total - one])
    sizes = jnp.asarray(length_profile(count, total, bound, skew), jnp.int32)
    twos = (count - 1) // 2
    giver, receiver = sizes[1:1 + 2 * twos:2], sizes[2:2 + 2 * twos:2]
    room = jnp.minimum(giver - 1, bound - receiver)
    passed = jax.random.randint(jax.random.fold_in(stream_key, 1), (twos,), 0, 1 << 20) % (room + 1)
    sizes = sizes.at[1:1 + 2 * twos:2].set(giver - passed).at[2:2 + 2 * twos:2].set(receiver + passed)
    return sizes[jax.random.permutation(jax.random.fold_in(stream_key, 2), count)]


def scatter_about(own_key, extent, width, bound, split=(), kind=jnp.bfloat16):
    drawn = width * jax.random.normal(own_key, extent, jnp.float32)
    if split:
        drawn = drawn * steps_of(own_key, extent, split, -0.22, 0.18)
    return jnp.clip(drawn, -bound, bound).astype(kind)


def setup_inputs(seed: int = 0) -> dict:
    arg_keys = jax.random.split(jax.random.key(seed), 12)
    return {
        "queries": draw_queries(jax.random.fold_in(arg_keys[11], 71), 0),
        "keys": draw_keys(jax.random.fold_in(arg_keys[11], 71), 0),
        "values": scatter_about(arg_keys[2], (FRAMES, FT, MODEL_DIM), 1.0, 6.0, ((0, 256),)),
        "residual": scatter_about(arg_keys[3], (FRAMES, FT, MODEL_DIM), 1.0, 6.0, ((0, 256),)),
        "target": scatter_about(arg_keys[4], (FRAMES, FT, MODEL_DIM), 1.0, 6.0, ((0, 256),)),
        "output_weight": scatter_about(arg_keys[5], (MODEL_DIM, MODEL_DIM), MODEL_DIM ** -0.5, 0.109375, ((0, 16),)),
        "down_adapter": scatter_about(arg_keys[6], (SCENE_COUNT, ADAPTER_RANK, MODEL_DIM), MODEL_DIM ** -0.5, 0.109375, ((0, 16), (2, 16))),
        "up_adapter": scatter_about(arg_keys[7], (SCENE_COUNT, ADAPTER_RANK, MODEL_DIM), 0.2, 1.1953125, ((0, 16), (2, 16))),
        "scene_of_frame": with_ends(ranked(arg_keys[8], (FRAMES,), SCENE_COUNT, 2), jax.random.fold_in(arg_keys[8], 3), 0, SCENE_COUNT - 1).astype(jnp.int32),
        "scene_adapter_row": jax.random.permutation(arg_keys[9], SCENE_COUNT).astype(jnp.int32),
        "valid_token_count": ragged(arg_keys[10], FRAMES, FRAMES * FT * 5 // 8, FT, 1).astype(jnp.int32),
    }


adapter_scale = 2.0

def attend_frame(query_frame, key_frame, value_frame, valid_mask):
    query_heads = query_frame.astype(jnp.float32).reshape(FT, HEADS, HD)
    key_heads = key_frame.astype(jnp.float32).reshape(FT, HEADS, HD)
    value_heads = value_frame.astype(jnp.float32).reshape(FT, HEADS, HD)
    scores = jnp.einsum('qhd,khd->hqk', query_heads, key_heads) * (1.0 / math.sqrt(HD))
    scores = jnp.where(valid_mask[None, None, :], scores, -jnp.inf)
    row_max = lax.optimization_barrier(jnp.max(scores, axis=-1, keepdims=True))
    exponent = jnp.exp(scores - row_max)
    weights = (exponent / lax.optimization_barrier(jnp.sum(exponent, axis=-1, keepdims=True))).astype(jnp.bfloat16)
    attended = jnp.einsum('hqk,khd->qhd', weights.astype(jnp.float32), value_heads)
    return attended.reshape(FT, MODEL_DIM).astype(jnp.bfloat16)

def reference(queries, keys, values, residual, target, output_weight, down_adapter, up_adapter, scene_of_frame, scene_adapter_row, valid_token_count):
    weight_wide = output_weight.astype(jnp.float32)
    slot_list = scene_adapter_row[scene_of_frame].astype(jnp.int32)

    def one_frame(running, inputs):
        query_frame, key_frame, value_frame, residual_frame, target_frame_value, token_total, adapter_slot_index = inputs
        valid_mask = jnp.arange(FT, dtype=jnp.int32) < token_total
        attended = attend_frame(query_frame, key_frame, value_frame, valid_mask)
        projected_tokens = jnp.dot(attended.astype(jnp.float32), weight_wide, preferred_element_type=jnp.float32)
        down_weight_rows = down_adapter[adapter_slot_index]
        up_weight_rows = up_adapter[adapter_slot_index]
        low_rank_state = jnp.dot(attended, down_weight_rows.T, preferred_element_type=jnp.float32).astype(jnp.bfloat16)
        adapter_output = jnp.dot(low_rank_state, up_weight_rows, preferred_element_type=jnp.float32)
        combined_output = residual_frame.astype(jnp.float32) + projected_tokens + adapter_scale * adapter_output - target_frame_value.astype(jnp.float32)
        residual_error = jnp.where(valid_mask[:, None], combined_output, jnp.zeros_like(combined_output))
        token_float = token_total.astype(jnp.float32)
        frame_loss = jnp.sum(residual_error * residual_error) / (token_float * MODEL_DIM)
        output_gradient = (2.0 * residual_error / token_float).astype(jnp.bfloat16)
        up_gradient_terms = adapter_scale * jnp.dot(low_rank_state.T, output_gradient, preferred_element_type=jnp.float32)
        backward_low_rank = (adapter_scale * jnp.dot(output_gradient, up_weight_rows.T, preferred_element_type=jnp.float32)).astype(jnp.bfloat16)
        down_terms = jnp.dot(backward_low_rank.T, attended, preferred_element_type=jnp.float32)
        sum_down, sum_up = running
        return ((sum_down.at[adapter_slot_index].add(down_terms), sum_up.at[adapter_slot_index].add(up_gradient_terms)), frame_loss)
    start_sums = (jnp.zeros((SCENE_COUNT, ADAPTER_RANK, MODEL_DIM), jnp.float32), jnp.zeros((SCENE_COUNT, ADAPTER_RANK, MODEL_DIM), jnp.float32))
    (grad_down, grad_up), frame_loss = lax.scan(one_frame, start_sums, (queries, keys, values, residual, target, valid_token_count, slot_list))
    return (grad_down, grad_up, frame_loss)
```

```python
import functools
import math

import jax
import jax.numpy as jnp
from jax import lax
from jax.experimental import pallas as pl
from jax.experimental.pallas import tpu as pltpu
from jax.sharding import PartitionSpec as P

HEADS = 24
HD = 128
FT = 192
D = 3072
RANK = 64
SC = 16
RB = D // 16
HALF = RB // 2
NB = 256
LANES = 128
K_OWN = 3
K_FAR = 4
MESH = pl.DeviceIdType.MESH
F32 = jnp.float32
BF16 = jnp.bfloat16
SCALE = 1.0 / math.sqrt(HD)


def dot(a, b, ca, cb):
    return lax.dot_general(a, b, (((ca,), (cb,)), ((), ())), preferred_element_type=F32)


class Sems:
    def __init__(self, send, recv):
        self.send, self.recv, self.count = send, recv, 0

    def take(self):
        self.count += 1
        return self.count - 1

    def copy(self, k, src, dst, dev):
        return pltpu.make_async_remote_copy(
            src_ref=src, dst_ref=dst, send_sem=self.send.at[k], recv_sem=self.recv.at[k],
            device_id=dev, device_id_type=MESH,
        )


N_SEMS = 256


def kernel(
    q_hbm, k_hbm, v_hbm, res_hbm, tgt_hbm, w_hbm, down_ref, up_ref, scene_ref, row_ref, count_ref,
    gd_ref, gu_ref, loss_ref,
    q, k, v, res, tgt, w, att, acc, cot, slots, bundle, gath, picked, du, terms, got, dense, dense16,
    xgot, xsum, xsum16, zgot, lvec, blvec, slot_sm, ssem, rsem, lsem,
):
    sems = Sems(ssem, rsem)
    i = lax.axis_index("frame")
    j = lax.axis_index("fsdp")
    x, zl = i // 4, i % 4
    hi, y, c = j // 8, (j // 2) % 4, j % 2
    far = 1 - hi
    edge = jnp.logical_or(zl == 0, zl == 3)
    inner_zl = jnp.where(zl == 0, 1, 2)

    def fs(h, yy, cc):
        return h * 8 + yy * 2 + cc

    def at_y(dy):
        return (i, fs(hi, (y + dy + 4) % 4, c))

    def at_x(dx):
        return (((x + dx + 4) % 4) * 4 + zl, j)

    partner = (x * 4 + 3 - zl, fs(far, y, c))
    twin = (i, j + 1 - 2 * c)

    barrier = pltpu.get_barrier_semaphore()
    peers = [(i, (j + d) % 16) for d in range(1, 16)]
    peers += [at_x(d) for d in range(1, 4)]
    peers += [(x * 4 + (zl + d) % 4, j) for d in range(1, 4)]
    peers += [partner]
    for peer in peers:
        pl.semaphore_signal(barrier, inc=1, device_id=peer, device_id_type=MESH)

    loads = []
    for n, (src, dst) in enumerate(((q_hbm, q), (k_hbm, k), (v_hbm, v), (res_hbm, res), (tgt_hbm, tgt))):
        cp = pltpu.make_async_copy(src.at[0], dst, lsem.at[n])
        cp.start()
        loads.append(cp)
    own_row = pl.multiple_of(j * RB, RB)
    own_load = pltpu.make_async_copy(w_hbm, w.at[pl.ds(own_row, RB)], lsem.at[5])
    own_load.start()

    pl.semaphore_wait(barrier, len(peers))

    def quarter(cls, xx):
        kk = K_OWN if cls == 0 else K_FAR
        return pl.ds(pl.multiple_of(xx * (kk * LANES), LANES), kk * LANES)

    def rest(cls):
        kk = K_OWN if cls == 0 else K_FAR
        return pl.ds(4 * kk * LANES, D - 4 * kk * LANES)

    def shard_row(h, yy):
        return pl.multiple_of(fs(h, yy, c) * RB, RB)

    def half_rows(h, yy, s):
        return pl.ds(pl.multiple_of(shard_row(h, yy) + s * HALF, HALF), HALF)

    sends = []

    def push(kk, src, dst, dev):
        cp = sems.copy(kk, src, dst, dev)
        cp.start()
        sends.append(cp)

    def arrived(kk, dst, dev):
        sems.copy(kk, dst, dst, dev).wait_recv()

    hs = (hi, far)

    y_id = [[[[sems.take() for _ in range(3)] for _ in range(2)] for _ in range(2)] for _ in range(2)]
    z_id = [[sems.take() for _ in range(2)] for _ in range(2)]
    shards = [(1, 0), (0, 1), (0, 3), (0, 2), (1, 1), (1, 3), (1, 2)]
    x_id = [[[sems.take() for _ in range(3)] for _ in range(2)] for _ in range(7)]
    die_id = [[sems.take() for _ in range(2)] for _ in range(8)]
    DIRS = (1, -1)

    def order(d):
        return (0, 1) if d == 1 else (1, 0)

    def cols_of(cls, piece):
        return quarter(cls, x) if piece == 0 else rest(cls)

    def y_send(cls, piece, from_hbm):
        for dn, d in enumerate(DIRS):
            for n, s in enumerate(order(d)):
                cols = cols_of(cls, piece)
                dst = w.at[half_rows(hs[cls], y, s), cols]
                src = w_hbm.at[pl.ds(s * HALF, HALF), cols] if from_hbm else dst
                push(y_id[cls][piece][dn][n], src, dst, at_y(d))

    def y_forward(cls, piece):
        for dn, d in enumerate(DIRS):
            s = order(d)[0]
            reg = w.at[half_rows(hs[cls], (y - d + 4) % 4, s), cols_of(cls, piece)]
            arrived(y_id[cls][piece][dn][0], reg, at_y(d))
            push(y_id[cls][piece][dn][2], reg, reg, at_y(d))

    def y_second(cls, piece, dn):
        d = DIRS[dn]
        s = order(d)[1]
        reg = w.at[half_rows(hs[cls], (y - d + 4) % 4, s), cols_of(cls, piece)]
        arrived(y_id[cls][piece][dn][1], reg, at_y(d))

    def y_last(cls, piece):
        for dn, d in enumerate(DIRS):
            s = order(d)[0]
            reg = w.at[half_rows(hs[cls], (y + 2) % 4, s), cols_of(cls, piece)]
            arrived(y_id[cls][piece][dn][2], reg, at_y(d))

    def x_send(n):
        cls, dy = shards[n]
        for dn, d in enumerate(DIRS):
            for m, s in enumerate(order(d)):
                reg = w.at[half_rows(hs[cls], (y + dy) % 4, s), quarter(cls, x)]
                push(x_id[n][dn][m], reg, reg, at_x(d))

    def x_forward(n):
        cls, dy = shards[n]
        for dn, d in enumerate(DIRS):
            s = order(d)[0]
            reg = w.at[half_rows(hs[cls], (y + dy) % 4, s), quarter(cls, (x - d + 4) % 4)]
            arrived(x_id[n][dn][0], reg, at_x(d))
            push(x_id[n][dn][2], reg, reg, at_x(d))

    def x_finish(n):
        cls, dy = shards[n]
        for dn, d in enumerate(DIRS):
            s = order(d)[1]
            reg = w.at[half_rows(hs[cls], (y + dy) % 4, s), quarter(cls, (x - d + 4) % 4)]
            arrived(x_id[n][dn][1], reg, at_x(d))
            s = order(d)[0]
            reg = w.at[half_rows(hs[cls], (y + dy) % 4, s), quarter(cls, (x + 2) % 4)]
            arrived(x_id[n][dn][2], reg, at_x(d))

    def z_cols(p):
        return quarter(1, x) if p == 0 else rest(1)

    def z_start():
        @pl.when(edge)
        def _():
            for p in range(2):
                sems.copy(
                    z_id[p][0], w_hbm.at[:, z_cols(p)], w.at[pl.ds(own_row, RB), z_cols(p)], partner
                ).start()

    far_rows = pl.ds(shard_row(far, y), RB)

    def z_take(p):
        reg = w.at[far_rows, z_cols(p)]

        @pl.when(edge)
        def _():
            arrived(z_id[p][0], reg, partner)
            sems.copy(z_id[p][1], reg, reg, (x * 4 + inner_zl, j)).start()

        @pl.when(jnp.logical_not(edge))
        def _():
            arrived(z_id[p][1], reg, partner)

    def z_done():
        @pl.when(edge)
        def _():
            for p in range(2):
                reg = w.at[far_rows, z_cols(p)]
                sems.copy(z_id[p][0], w_hbm.at[:, z_cols(p)], reg, partner).wait_send()
                sems.copy(z_id[p][1], reg, reg, partner).wait_send()

    mul_order = [(0, 0), (0, 1), (0, 3), (0, 2), (1, 0), (1, 1), (1, 3), (1, 2)]

    def die_send(m):
        cls, dy = mul_order[m]
        for s in range(2):
            dst = w.at[half_rows(hs[cls], (y + dy) % 4, s)]
            src = w_hbm.at[pl.ds(s * HALF, HALF)] if m == 0 else dst
            push(die_id[m][s], src, dst, twin)

    def die_take(m):
        cls, dy = mul_order[m]
        for s in range(2):
            r = pl.multiple_of(fs(hs[cls], (y + dy) % 4, 1 - c) * RB + s * HALF, HALF)
            arrived(die_id[m][s], w.at[pl.ds(r, HALF)], twin)

    count = count_ref[0]

    def heads(lo, up):
        def one(h, carry):
            cols = pl.ds(pl.multiple_of(h * HD, HD), HD)
            s = dot(q[:, cols], k[:, cols], 1, 1) * SCALE
            pos = lax.broadcasted_iota(jnp.int32, (FT, FT), 1)
            s = jnp.where(pos < count, s, -jnp.inf)
            e = jnp.exp(s - jnp.max(s, axis=1, keepdims=True))
            p = (e / jnp.sum(e, axis=1, keepdims=True)).astype(BF16)
            att[:, cols] = dot(p, v[:, cols], 1, 0).astype(BF16)
            return carry

        lax.fori_loop(lo, up, one, 0)

    def multiply(m):
        cls, dy = mul_order[m]
        r = pl.multiple_of(fs(hs[cls], (y + dy) % 4, 0) * RB, 2 * RB)
        a = att[:, pl.ds(r, 2 * RB)]

        def one(n, carry):
            cols = pl.ds(pl.multiple_of(n * NB, NB), NB)
            part = dot(a, w[pl.ds(r, 2 * RB), cols], 1, 0)
            if m == 0:
                acc[:, cols] = part
            else:
                acc[:, cols] += part
            return carry

        lax.fori_loop(0, D // NB, one, 0)

    z_start()
    y_send(0, 0, True)
    my_slot = row_ref[scene_ref[0]]
    slots[pl.ds(j, 1)] = jnp.full((1, 8, LANES), my_slot, jnp.int32)
    both = jnp.concatenate([down_ref[0].astype(F32), up_ref[0].astype(F32)], axis=0)
    both = jnp.concatenate([both, jnp.zeros((2 * RANK, 256 - RB), F32)], axis=1)
    bundle[...] = both.T[:RB].astype(BF16)
    gath[pl.ds(i, 1)] = bundle[...][None]
    slot_id = [sems.take() for _ in range(15)]
    gz_id = [sems.take() for _ in range(3)]
    gx_id = [sems.take() for _ in range(3)]
    pick_id = [sems.take() for _ in range(15)]
    term_id = [sems.take() for _ in range(15)]
    rx_id = [sems.take() for _ in range(3)]
    rz_id = [sems.take() for _ in range(3)]
    for d in range(1, 4):
        push(gz_id[d - 1], bundle, gath.at[i], (x * 4 + (zl + d) % 4, j))
    for d in range(1, 16):
        push(slot_id[d - 1], slots.at[j], slots.at[j], (i, (j + d) % 16))
    y_send(0, 1, True)
    die_send(0)

    for cp in loads[:3]:
        cp.wait()
    heads(0, 6)
    for d in range(1, 4):
        src = x * 4 + (zl - d + 4) % 4
        arrived(gz_id[d - 1], gath.at[src], (src, j))
    for d in range(1, 4):
        reg = gath.at[pl.ds(x * 4, 4)]
        push(gx_id[d - 1], reg, reg, at_x(d))
    y_forward(0, 0)
    for dn, n in ((0, 2), (1, 1)):
        y_second(0, 0, dn)
        x_send(n)
    z_take(0)
    y_send(1, 0, False)
    x_send(0)
    heads(6, 14)
    y_last(0, 0)
    x_send(3)
    y_forward(1, 0)
    for dn, n in ((0, 5), (1, 4)):
        y_second(1, 0, dn)
        x_send(n)
    x_forward(2)
    x_forward(1)
    heads(14, 24)
    for d in range(1, 16):
        arrived(slot_id[d - 1], slots.at[(j - d + 16) % 16], twin)
    for d in range(1, 4):
        src = pl.ds(((x - d + 4) % 4) * 4, 4)
        arrived(gx_id[d - 1], gath.at[src], at_x(d))
    for f in range(16):
        slot_sm[f] = jnp.max(slots[f])
    for f in range(16):
        picked[f] = gath[slot_sm[f]]
    for d in range(1, 16):
        to = (j + d) % 16
        push(pick_id[d - 1], picked.at[to], du.at[j], (i, to))
    du[pl.ds(j, 1)] = picked[pl.ds(j, 1)]
    x_forward(0)
    y_last(1, 0)
    x_send(6)
    z_take(1)
    y_send(1, 1, False)
    y_forward(0, 1)
    own_load.wait()
    die_take(0)
    multiply(0)
    x_forward(3)
    x_forward(5)
    x_forward(4)
    for dn in range(2):
        y_second(0, 1, dn)
    x_finish(2)
    x_finish(1)
    die_send(1)
    die_send(2)
    die_take(1)
    multiply(1)
    die_take(2)
    multiply(2)
    y_last(0, 1)
    x_finish(3)
    die_send(3)
    x_finish(0)
    die_send(4)
    x_forward(6)
    die_take(3)
    multiply(3)
    die_take(4)
    multiply(4)
    y_forward(1, 1)
    for d in range(1, 16):
        arrived(pick_id[d - 1], du.at[(j - d + 16) % 16], twin)

    lane = lax.broadcasted_iota(jnp.int32, (FT, LANES), 1)

    def low(n, total):
        return total + dot(
            att[:, pl.ds(pl.multiple_of(n * 384, 384), 384)],
            du[pl.ds(n * 2, 2)].reshape(384, LANES), 1, 0,
        )

    lr = lax.fori_loop(0, 8, low, jnp.zeros((FT, LANES), F32)).astype(BF16).astype(F32)
    lr_low = jnp.where(lane < RANK, 2.0 * lr, 0.0)
    l_low = lr_low.astype(BF16)
    l_high = pltpu.roll(lr_low, RANK, 1).astype(BF16)
    lvec[0] = l_low
    lvec[1] = l_high
    for cp in loads[3:]:
        cp.wait()
    row = lax.broadcasted_iota(jnp.int32, (FT, 1), 0)
    valid = row < count

    for dn in range(2):
        y_second(1, 1, dn)
    x_finish(5)
    x_finish(4)
    die_send(5)
    die_send(6)
    die_take(5)
    multiply(5)
    die_take(6)
    multiply(6)
    y_last(1, 1)
    x_finish(6)
    die_send(7)
    die_take(7)
    multiply(7)

    inv = 2.0 / count.astype(F32)
    ND = 384

    def back(n, carry):
        loss, bl = carry
        cols = pl.ds(pl.multiple_of(n * ND, ND), ND)
        dn_ = du[pl.ds(n * 2, 2)].reshape(ND, LANES)
        e = (
            res[:, cols].astype(F32) + acc[:, cols] + dot(lvec[1], dn_, 1, 1)
            - tgt[:, cols].astype(F32)
        )
        e = jnp.where(valid, e, 0.0)
        loss = loss + jnp.sum((e * e).reshape(FT // 8, 8, ND), axis=0)
        ct = (inv * e).astype(BF16)
        cot[:, cols] = ct
        bl = bl + dot(ct, dn_, 1, 0)
        return loss, bl

    loss, bl = lax.fori_loop(
        0, D // ND, back, (jnp.zeros((8, ND), F32), jnp.zeros((FT, LANES), F32))
    )
    loss_ref[0] = jnp.sum(loss) / (count.astype(F32) * D)
    blvec[...] = jnp.where(lane < RANK, 0.0, 2.0 * bl).astype(BF16)

    def term(n, carry):
        cols = pl.ds(pl.multiple_of(n * ND, ND), ND)
        t = dot(lvec[0], cot[:, cols], 0, 0) + dot(blvec[...], att[:, cols], 0, 0)
        terms[pl.ds(n * 2, 2)] = t.T.reshape(2, RB, LANES).astype(BF16)
        return carry

    lax.fori_loop(0, D // ND, term, 0)
    for d in range(1, 16):
        to = (j + d) % 16
        push(term_id[d - 1], terms.at[to], got.at[j], (i, to))
    got[pl.ds(j, 1)] = terms[pl.ds(j, 1)]
    for d in range(1, 16):
        arrived(term_id[d - 1], got.at[(j - d + 16) % 16], twin)

    def sums(n, carry):
        rows = pl.ds(pl.multiple_of(n * 16, 16), 16)
        parts = [got[f, rows].astype(F32) for f in range(16)]
        for s in range(SC):
            total = jnp.zeros((16, LANES), F32)
            for f in range(16):
                total = total + jnp.where(slot_sm[f] == s, 1.0, 0.0) * parts[f]
            dense[s, rows] = total
            dense16[s, rows] = total.astype(BF16)
        return carry

    lax.fori_loop(0, RB // 16, sums, 0)
    for d in range(1, 4):
        to = (x + d) % 4
        push(rx_id[d - 1], dense16.at[pl.ds(to * 4, 4)], xgot.at[d - 1], at_x(d))
    for d in range(1, 4):
        arrived(rx_id[d - 1], xgot.at[d - 1], at_x(d))
    for s in range(4):
        total = dense[pl.ds(x * 4 + s, 1)][0]
        for d in range(3):
            total = total + xgot[d, s].astype(F32)
        xsum[s] = total
        xsum16[s] = total.astype(BF16)
    for d in range(1, 4):
        to = (zl + d) % 4
        push(rz_id[d - 1], xsum16.at[to], zgot.at[d - 1], (x * 4 + to, j))
    for d in range(1, 4):
        arrived(rz_id[d - 1], zgot.at[d - 1], twin)
    total = xsum[pl.ds(zl, 1)][0]
    for d in range(3):
        total = total + zgot[d].astype(F32)
    final = jnp.concatenate([total, jnp.zeros((256 - RB, LANES), F32)], axis=0).T
    gu_ref[0] = final[:RANK, :RB]
    gd_ref[0] = final[RANK:, :RB]

    for cp in sends:
        cp.wait_send()
    z_done()


def per_device(*args):
    anyspec = pl.BlockSpec(memory_space=pl.ANY)
    vm = pl.BlockSpec(memory_space=pltpu.VMEM)
    sm = pl.BlockSpec(memory_space=pltpu.SMEM)
    big = pltpu.VMEM((FT, D), BF16)
    block = lambda *lead: pltpu.VMEM((*lead, RB, LANES), BF16)
    return pl.pallas_call(
        kernel,
        out_shape=(
            jax.ShapeDtypeStruct((1, RANK, RB), F32),
            jax.ShapeDtypeStruct((1, RANK, RB), F32),
            jax.ShapeDtypeStruct((1,), F32),
        ),
        in_specs=[anyspec] * 6 + [vm] * 2 + [sm] * 3,
        out_specs=(vm, vm, sm),
        scratch_shapes=[
            big, big, big, big, big,
            pltpu.VMEM((D, D), BF16),
            big,
            pltpu.VMEM((FT, D), F32),
            big,
            pltpu.VMEM((16, 8, LANES), jnp.int32),
            block(), block(16), block(16), block(16), block(16), block(16),
            pltpu.VMEM((16, RB, LANES), F32),
            block(16), block(3, 4),
            pltpu.VMEM((4, RB, LANES), F32),
            block(4), block(3),
            pltpu.VMEM((2, FT, LANES), BF16),
            pltpu.VMEM((FT, LANES), BF16),
            pltpu.SMEM((16,), jnp.int32),
            pltpu.SemaphoreType.DMA((N_SEMS,)),
            pltpu.SemaphoreType.DMA((N_SEMS,)),
            pltpu.SemaphoreType.DMA((8,)),
        ],
        compiler_params=pltpu.CompilerParams(
            collective_id=0, has_side_effects=True, vmem_limit_bytes=60 * 2**20
        ),
        name="step",
    )(*args)


def solution(mesh):
    wide = P(("frame", "fsdp"), None, None)
    flat = P(("frame", "fsdp"))
    adapter = P("frame", None, "fsdp")
    return jax.shard_map(
        per_device,
        mesh=mesh,
        in_specs=(wide,) * 5 + (P("fsdp", None), adapter, adapter, flat, P(), flat),
        out_specs=(adapter, adapter, flat),
        check_vma=False,
    )
```

```python
import functools
import math

import jax
import jax.numpy as jnp
from jax import lax
from jax.experimental import pallas as pl
from jax.experimental.pallas import tpu as pltpu
from jax.sharding import PartitionSpec as P

HEADS = 24
HD = 128
FT = 192
D = 3072
RANK = 64
SC = 16
RB = D // 16
HALF = RB // 2
NB = 256
LANES = 128
K_OWN = 4
K_FAR = 4
MESH = pl.DeviceIdType.MESH
F32 = jnp.float32
BF16 = jnp.bfloat16
SCALE = 1.0 / math.sqrt(HD)


def dot(a, b, ca, cb):
    return lax.dot_general(a, b, (((ca,), (cb,)), ((), ())), preferred_element_type=F32)


class Sems:
    def __init__(self, send, recv):
        self.send, self.recv, self.count = send, recv, 0

    def take(self):
        self.count += 1
        return self.count - 1

    def copy(self, k, src, dst, dev):
        return pltpu.make_async_remote_copy(
            src_ref=src, dst_ref=dst, send_sem=self.send.at[k], recv_sem=self.recv.at[k],
            device_id=dev, device_id_type=MESH,
        )


N_SEMS = 256


class Phase:
    def __init__(self):
        self.scope = None

    def __call__(self, name):
        if self.scope is not None:
            self.scope.__exit__(None, None, None)
        self.scope = None
        if name:
            self.scope = jax.named_scope(name)
            self.scope.__enter__()


def kernel(
    q_hbm, k_hbm, v_hbm, res_hbm, tgt_hbm, w_hbm, down_ref, up_ref, scene_ref, row_ref, count_ref,
    gd_ref, gu_ref, loss_ref,
    q, k, v, res, tgt, w, att, acc, cot, slots, bundle, gath, picked, du, terms, got, dense, dense16,
    xgot, xsum, xsum16, zgot, lvec, lhigh, blvec, slot_sm, ssem, rsem, lsem,
):
    phase = Phase()
    phase("entry")
    sems = Sems(ssem, rsem)
    i = lax.axis_index("frame")
    j = lax.axis_index("fsdp")
    x, zl = i // 4, i % 4
    hi, y, c = j // 8, (j // 2) % 4, j % 2
    far = 1 - hi
    edge = jnp.logical_or(zl == 0, zl == 3)
    inner_zl = jnp.where(zl == 0, 1, 2)

    def fs(h, yy, cc):
        return h * 8 + yy * 2 + cc

    def at_y(dy):
        return (i, fs(hi, (y + dy + 4) % 4, c))

    def at_x(dx):
        return (((x + dx + 4) % 4) * 4 + zl, j)

    partner = (x * 4 + 3 - zl, fs(far, y, c))
    twin = (i, j + 1 - 2 * c)

    barrier = pltpu.get_barrier_semaphore()
    peers = [(i, (j + d) % 16) for d in range(1, 16)]
    peers += [at_x(d) for d in range(1, 4)]
    peers += [(x * 4 + (zl + d) % 4, j) for d in range(1, 4)]
    peers += [partner]
    for peer in peers:
        pl.semaphore_signal(barrier, inc=1, device_id=peer, device_id_type=MESH)

    loads = []
    for n, (src, dst) in enumerate(((q_hbm, q), (k_hbm, k), (v_hbm, v), (res_hbm, res), (tgt_hbm, tgt))):
        cp = pltpu.make_async_copy(src.at[0], dst, lsem.at[n])
        cp.start()
        loads.append(cp)
    own_row = pl.multiple_of(j * RB, RB)
    own_load = pltpu.make_async_copy(w_hbm, w.at[pl.ds(own_row, RB)], lsem.at[5])
    own_load.start()

    phase("barrier")
    pl.semaphore_wait(barrier, len(peers))

    def quarter(cls, xx):
        kk = K_OWN if cls == 0 else K_FAR
        return pl.ds(pl.multiple_of(xx * (kk * LANES), LANES), kk * LANES)

    def rest(cls, part):
        kk = K_OWN if cls == 0 else K_FAR
        size = (D - 4 * kk * LANES) // 2
        return pl.ds(4 * kk * LANES + part * size, size)

    def shard_row(h, yy):
        return pl.multiple_of(fs(h, yy, c) * RB, RB)

    def half_rows(h, yy, s):
        return pl.ds(pl.multiple_of(shard_row(h, yy) + s * HALF, HALF), HALF)

    sends = []

    def push(kk, src, dst, dev):
        cp = sems.copy(kk, src, dst, dev)
        cp.start()
        sends.append(cp)

    def arrived(kk, dst, dev):
        sems.copy(kk, dst, dst, dev).wait_recv()

    hs = (hi, far)

    y_id = [[[[sems.take() for _ in range(3)] for _ in range(2)] for _ in range(3)] for _ in range(2)]
    z_id = [[sems.take() for _ in range(2)] for _ in range(3)]
    shards = [(1, 0), (0, 1), (0, 3), (0, 2), (1, 1), (1, 3), (1, 2)]
    x_id = [[[sems.take() for _ in range(3)] for _ in range(2)] for _ in range(7)]
    die_id = [[sems.take() for _ in range(2)] for _ in range(8)]
    DIRS = (1, -1)

    def order(d):
        return (0, 1) if d == 1 else (1, 0)

    def cols_of(cls, piece):
        return quarter(cls, x) if piece == 0 else rest(cls, piece - 1)

    def y_send(cls, piece, from_hbm):
        for dn, d in enumerate(DIRS):
            for n, s in enumerate(order(d)):
                cols = cols_of(cls, piece)
                dst = w.at[half_rows(hs[cls], y, s), cols]
                src = w_hbm.at[pl.ds(s * HALF, HALF), cols] if from_hbm else dst
                push(y_id[cls][piece][dn][n], src, dst, at_y(d))

    def y_forward(cls, piece):
        for dn, d in enumerate(DIRS):
            s = order(d)[0]
            reg = w.at[half_rows(hs[cls], (y - d + 4) % 4, s), cols_of(cls, piece)]
            arrived(y_id[cls][piece][dn][0], reg, at_y(d))
            push(y_id[cls][piece][dn][2], reg, reg, at_y(d))

    def y_second(cls, piece, dn):
        d = DIRS[dn]
        s = order(d)[1]
        reg = w.at[half_rows(hs[cls], (y - d + 4) % 4, s), cols_of(cls, piece)]
        arrived(y_id[cls][piece][dn][1], reg, at_y(d))

    def y_last(cls, piece):
        for dn, d in enumerate(DIRS):
            s = order(d)[0]
            reg = w.at[half_rows(hs[cls], (y + 2) % 4, s), cols_of(cls, piece)]
            arrived(y_id[cls][piece][dn][2], reg, at_y(d))

    def x_send(n):
        cls, dy = shards[n]
        for dn, d in enumerate(DIRS):
            for m, s in enumerate(order(d)):
                reg = w.at[half_rows(hs[cls], (y + dy) % 4, s), quarter(cls, x)]
                push(x_id[n][dn][m], reg, reg, at_x(d))

    def x_forward(n):
        cls, dy = shards[n]
        for dn, d in enumerate(DIRS):
            s = order(d)[0]
            reg = w.at[half_rows(hs[cls], (y + dy) % 4, s), quarter(cls, (x - d + 4) % 4)]
            arrived(x_id[n][dn][0], reg, at_x(d))
            push(x_id[n][dn][2], reg, reg, at_x(d))

    def x_finish(n):
        cls, dy = shards[n]
        for dn, d in enumerate(DIRS):
            s = order(d)[1]
            reg = w.at[half_rows(hs[cls], (y + dy) % 4, s), quarter(cls, (x - d + 4) % 4)]
            arrived(x_id[n][dn][1], reg, at_x(d))
            s = order(d)[0]
            reg = w.at[half_rows(hs[cls], (y + dy) % 4, s), quarter(cls, (x + 2) % 4)]
            arrived(x_id[n][dn][2], reg, at_x(d))

    def z_cols(p):
        return cols_of(1, p)

    def z_start():
        @pl.when(edge)
        def _():
            for p in range(3):
                sems.copy(
                    z_id[p][0], w_hbm.at[:, z_cols(p)], w.at[pl.ds(own_row, RB), z_cols(p)], partner
                ).start()

    far_rows = pl.ds(shard_row(far, y), RB)

    def z_edge(p):
        reg = w.at[far_rows, z_cols(p)]

        @pl.when(edge)
        def _():
            arrived(z_id[p][0], reg, partner)
            sems.copy(z_id[p][1], reg, reg, (x * 4 + inner_zl, j)).start()

    def z_inner(p):
        reg = w.at[far_rows, z_cols(p)]

        @pl.when(jnp.logical_not(edge))
        def _():
            arrived(z_id[p][1], reg, partner)

    def z_done():
        @pl.when(edge)
        def _():
            for p in range(3):
                reg = w.at[far_rows, z_cols(p)]
                sems.copy(z_id[p][0], w_hbm.at[:, z_cols(p)], reg, partner).wait_send()
                sems.copy(z_id[p][1], reg, reg, partner).wait_send()

    mul_order = [(0, 0), (0, 1), (0, 3), (0, 2), (1, 0), (1, 1), (1, 3), (1, 2)]

    cut = 4 * K_FAR * LANES
    die_cols = (pl.ds(0, cut), pl.ds(cut, D - cut))

    def die_send(m, p):
        cls, dy = mul_order[m]
        dst = w.at[pl.ds(shard_row(hs[cls], (y + dy) % 4), RB), die_cols[p]]
        src = w_hbm.at[:, die_cols[p]] if m == 0 else dst
        push(die_id[m][p], src, dst, twin)

    def die_take(m):
        cls, dy = mul_order[m]
        r = pl.multiple_of(fs(hs[cls], (y + dy) % 4, 1 - c) * RB, RB)
        for p in range(2):
            arrived(die_id[m][p], w.at[pl.ds(r, RB), die_cols[p]], twin)

    count = count_ref[0]

    def heads(lo, up):
        def one(h, carry):
            cols = pl.ds(pl.multiple_of(h * HD, HD), HD)
            s = dot(q[:, cols], k[:, cols], 1, 1) * SCALE
            pos = lax.broadcasted_iota(jnp.int32, (FT, FT), 1)
            s = jnp.where(pos < count, s, -jnp.inf)
            e = jnp.exp(s - jnp.max(s, axis=1, keepdims=True))
            p = (e / jnp.sum(e, axis=1, keepdims=True)).astype(BF16)
            att[:, cols] = dot(p, v[:, cols], 1, 0).astype(BF16)
            return carry

        lax.fori_loop(lo, up, one, 0)

    def pair_row(m):
        cls, dy = mul_order[m]
        return pl.multiple_of(fs(hs[cls], (y + dy) % 4, 0) * RB, 2 * RB)

    def multiply(*group):
        def one(n, carry):
            cols = pl.ds(pl.multiple_of(n * NB, NB), NB)
            total = None if group[0] == 0 else acc[:, cols]
            for m in group:
                rows = pl.ds(pair_row(m), 2 * RB)
                part = dot(att[:, rows], w[rows, cols], 1, 0)
                total = part if total is None else total + part
            acc[:, cols] = total
            return carry

        lax.fori_loop(0, D // NB, one, 0)

    phase("start")
    z_start()
    y_send(0, 0, True)
    my_slot = row_ref[scene_ref[0]]
    slots[pl.ds(j, 1)] = jnp.full((1, 8, LANES), my_slot, jnp.int32)
    both = jnp.concatenate([down_ref[0].astype(F32), up_ref[0].astype(F32)], axis=0)
    both = jnp.concatenate([both, jnp.zeros((2 * RANK, 256 - RB), F32)], axis=1)
    bundle[...] = both.T[:RB].astype(BF16)
    gath[pl.ds(zl * 4 + x, 1)] = bundle[...][None]

    def gz_copy(dn, t):
        d = DIRS[dn]
        reg = gath.at[pl.ds((zl - d * t) * 4, 4)]
        return sems.copy(gz_id[dn][t], reg, reg, (x * 4 + zl + d, j))

    def gz_has(dn, t):
        return zl >= t if dn == 0 else zl <= 3 - t

    def gz_goes(dn, t):
        return jnp.logical_and(gz_has(dn, t), zl < 3 if dn == 0 else zl > 0)

    def gz_hop(t):
        for dn in range(2):
            @pl.when(gz_goes(dn, t))
            def _():
                gz_copy(dn, t).start()

    def gz_take(t):
        for dn in range(2):
            @pl.when(gz_has(dn, t + 1))
            def _():
                reg = gath.at[pl.ds((zl - DIRS[dn] * (t + 1)) * 4, 4)]
                arrived(gz_id[dn][t], reg, twin)

    def gz_done():
        for t in range(3):
            for dn in range(2):
                @pl.when(gz_goes(dn, t))
                def _():
                    gz_copy(dn, t).wait_send()

    slot_id = [sems.take() for _ in range(15)]
    gz_id = [[sems.take() for _ in range(3)] for _ in range(2)]
    gx_id = [sems.take() for _ in range(3)]
    pick_id = [sems.take() for _ in range(15)]
    term_id = [[[sems.take() for _ in range(2)] for _ in range(8)] for _ in range(2)]
    rx_id = [[sems.take() for _ in range(3)] for _ in range(2)]
    rz_id = [[sems.take() for _ in range(3)] for _ in range(2)]
    for d in (2, 1, 3):
        push(gx_id[d - 1], bundle, gath.at[zl * 4 + x], at_x(d))
    for d in range(1, 16):
        push(slot_id[d - 1], slots.at[j], slots.at[j], (i, (j + d) % 16))
    y_send(0, 1, True)
    die_send(0, 0)
    die_send(0, 1)

    phase("h0_6")
    for cp in loads[:3]:
        cp.wait()
    heads(0, 6)
    phase("yf00")
    y_forward(0, 0)
    for dn, n in ((0, 2), (1, 1)):
        y_second(0, 0, dn)
        x_send(n)
    phase("ze0")
    z_edge(0)
    for d in range(1, 4):
        arrived(gx_id[d - 1], gath.at[zl * 4 + (x - d + 4) % 4], at_x(d))
    gz_hop(0)
    phase("h6_12")
    heads(6, 12)
    phase("zi0")
    z_inner(0)
    y_send(1, 0, False)
    x_send(0)
    y_send(0, 2, True)
    phase("yl00")
    y_last(0, 0)
    x_send(3)
    phase("yf01")
    y_forward(0, 1)
    phase("ze1")
    z_edge(1)
    gz_take(0)
    gz_hop(1)
    phase("h12_16")
    heads(12, 16)
    phase("xf21")
    x_forward(2)
    x_forward(1)
    phase("yf10")
    y_forward(1, 0)
    for dn, n in ((0, 5), (1, 4)):
        y_second(1, 0, dn)
        x_send(n)
    phase("ze2")
    z_edge(2)
    gz_take(1)
    gz_hop(2)
    phase("h16_20")
    heads(16, 20)
    phase("zi1")
    z_inner(1)
    y_send(1, 1, False)
    phase("xf0")
    x_forward(0)
    phase("h20_24")
    heads(20, 24)
    phase("xf3")
    x_forward(3)
    phase("yf02")
    y_forward(0, 2)
    phase("zi2")
    z_inner(2)
    y_send(1, 2, False)
    phase("slotgz")
    for d in range(1, 16):
        arrived(slot_id[d - 1], slots.at[(j - d + 16) % 16], twin)
    gz_take(2)
    phase("pick")
    for f in range(16):
        slot_sm[f] = jnp.max(slots[f])
    for f in range(16):
        picked[f] = gath[(slot_sm[f] % 4) * 4 + slot_sm[f] // 4]
    for d in (8, 7, 9, 6, 10, 5, 11, 4, 12, 3, 13, 2, 14, 1, 15):
        to = (j + d) % 16
        push(pick_id[d - 1], picked.at[to], du.at[j], (i, to))
    du[pl.ds(j, 1)] = picked[pl.ds(j, 1)]
    phase("yl10")
    y_last(1, 0)
    x_send(6)
    phase("mul0")
    own_load.wait()
    die_take(0)
    multiply(0)
    phase("yf11")
    y_forward(1, 1)
    phase("fin12")
    for dn in range(2):
        y_second(0, 1, dn)
        y_second(0, 2, dn)
    die_send(1, 1)
    die_send(2, 1)
    x_finish(2)
    x_finish(1)
    die_send(1, 0)
    die_send(2, 0)
    phase("xf54")
    x_forward(5)
    x_forward(4)
    phase("mul12")
    die_take(1)
    die_take(2)
    multiply(1, 2)
    phase("fin34")
    y_last(0, 1)
    y_last(0, 2)
    die_send(3, 1)
    die_send(4, 1)
    x_finish(0)
    die_send(4, 0)
    x_finish(3)
    die_send(3, 0)
    phase("yf12")
    y_forward(1, 2)
    phase("xf6")
    x_forward(6)
    phase("mul34")
    die_take(3)
    die_take(4)
    multiply(3, 4)
    phase("ys1")
    for dn in range(2):
        y_second(1, 1, dn)
        y_second(1, 2, dn)
    die_send(5, 1)
    die_send(6, 1)
    phase("xfin54")
    x_finish(5)
    die_send(6, 0)
    x_finish(4)
    die_send(5, 0)
    phase("pickwait")
    for d in range(1, 16):
        arrived(pick_id[d - 1], du.at[(j - d + 16) % 16], twin)
    phase("low")
    lane = lax.broadcasted_iota(jnp.int32, (FT, LANES), 1)

    def low(n, total):
        return total + dot(
            att[:, pl.ds(pl.multiple_of(n * 384, 384), 384)],
            du[pl.ds(n * 2, 2)].reshape(384, LANES), 1, 0,
        )

    lr = lax.fori_loop(0, 8, low, jnp.zeros((FT, LANES), F32)).astype(BF16).astype(F32)
    lr = jnp.where(lane < RANK, 2.0 * lr, 0.0)
    lvec[...] = lr[:, :RANK].astype(BF16)
    lhigh[...] = pltpu.roll(lr, RANK, 1).astype(BF16)
    for cp in loads[3:]:
        cp.wait()
    row = lax.broadcasted_iota(jnp.int32, (FT, 1), 0)
    valid = row < count
    phase("yl1")
    y_last(1, 1)
    y_last(1, 2)
    die_send(7, 1)
    phase("die56")
    die_take(5)
    die_take(6)
    phase("mul56")
    multiply(5, 6)
    phase("fin7")
    x_finish(6)
    die_send(7, 0)
    phase("die7")
    die_take(7)
    phase("back")
    inv = 2.0 / count.astype(F32)
    ND = 2 * RB
    chip = j // 2
    half_lane = lax.broadcasted_iota(jnp.int32, (32, LANES), 1) < 64
    last_rows = pl.ds(pair_row(7), 2 * RB)
    a_last = att[:, last_rows]

    def ship(h, step, n, t):
        top, bottom = t[:32, 128:256], t[32:, 128:256]
        packs = (
            (t[:, :128], jnp.where(half_lane, top, pltpu.roll(bottom, 64, 1))),
            (t[:, 256:], jnp.where(half_lane, pltpu.roll(top, 64, 1), bottom)),
        )
        for b in range(2):
            terms[h, pl.ds(n * 2 + b, 1), :64] = packs[b][0].astype(BF16)[None]
            terms[h, pl.ds(n * 2 + b, 1), 64:] = packs[b][1].astype(BF16)[None]
        for rel in range(2):
            to = n * 2 + (c + rel) % 2
            if step == 0 and rel == 0:
                got[h, pl.ds(j, 1)] = terms[h, pl.ds(j, 1)]
            else:
                push(term_id[h][step][rel], terms.at[h, to], got.at[h, j], (i, to))

    def terms_arrived(h):
        for step in (4, 3, 5, 2, 6, 1, 7, 0):
            for rel in range(2):
                if step == 0 and rel == 0:
                    continue
                src = ((chip - step + 8) % 8) * 2 + (c + rel) % 2
                arrived(term_id[h][step][rel], got.at[h, src], twin)

    loss = jnp.zeros((8, ND), F32)
    bl = jnp.zeros((FT, LANES), F32)
    for step in (4, 3, 5, 2, 6, 1, 7, 0):
        n = (chip + step) % 8
        cols = pl.ds(pl.multiple_of(n * ND, ND), ND)
        dn_ = du[pl.ds(n * 2, 2)].reshape(ND, LANES)
        e = acc[:, cols] + dot(a_last, w[last_rows, cols], 1, 0) + dot(lhigh[...], dn_, 1, 1)
        e = e + res[:, cols].astype(F32) - tgt[:, cols].astype(F32)
        e = jnp.where(valid, e, 0.0)
        loss = loss + jnp.sum((e * e).reshape(FT // 8, 8, ND), axis=0)
        ct = (inv * e).astype(BF16)
        bl = bl + dot(ct, dn_, 1, 0)
        ship(0, step, n, dot(lvec[...], ct, 0, 0))
    phase("down")
    blvec[...] = pltpu.roll(2.0 * bl, RANK, 1)[:, :RANK].astype(BF16)
    for step in (4, 3, 5, 2, 6, 1, 7, 0):
        n = (chip + step) % 8
        cols = pl.ds(pl.multiple_of(n * ND, ND), ND)
        ship(1, step, n, dot(blvec[...], att[:, cols], 0, 0))
    loss_ref[0] = jnp.sum(loss) / (count.astype(F32) * D)

    def slot_sums(h):
        def one(n, carry):
            rows = pl.ds(pl.multiple_of(n * 16, 16), 16)
            parts = [got[h, f, rows].astype(F32) for f in range(16)]
            for s in range(SC):
                total = jnp.zeros((16, LANES), F32)
                for f in range(16):
                    total = total + jnp.where(slot_sm[f] == s, 1.0, 0.0) * parts[f]
                dense[h, s, rows] = total
                dense16[h, s, rows] = total.astype(BF16)
            return carry

        lax.fori_loop(0, HALF // 16, one, 0)
        for d in (2, 1, 3):
            to = (x + d) % 4
            push(rx_id[h][d - 1], dense16.at[h, pl.ds(to * 4, 4)], xgot.at[h, d - 1], at_x(d))

    def x_sums(h):
        for d in range(1, 4):
            arrived(rx_id[h][d - 1], xgot.at[h, d - 1], at_x(d))
        for s in range(4):
            total = dense[h, pl.ds(x * 4 + s, 1)][0]
            for d in range(3):
                total = total + xgot[h, d, s].astype(F32)
            xsum[h, s] = total
            xsum16[h, s] = total.astype(BF16)
        for d in range(1, 4):
            to = (zl + d) % 4
            push(rz_id[h][d - 1], xsum16.at[h, to], zgot.at[h, d - 1], (x * 4 + to, j))

    def finish(h, out):
        for d in range(1, 4):
            arrived(rz_id[h][d - 1], zgot.at[h, d - 1], twin)
        total = xsum[h, pl.ds(zl, 1)][0]
        for d in range(3):
            total = total + zgot[h, d].astype(F32)
        wide = total[:64]
        thin = total[64:]
        thin = jnp.concatenate([thin, pltpu.roll(thin, 64, 1)], axis=0)
        turned = pltpu.roll(wide, 64, 1)
        lanes = lax.broadcasted_iota(jnp.int32, (64, LANES), 1)
        even = jnp.concatenate([wide, thin], axis=1)
        odd = jnp.concatenate([jnp.where(lanes < 64, thin, turned), turned], axis=1)
        out[0] = jnp.where(c == 0, even, odd)[:, :RB]

    phase("a2aup")
    terms_arrived(0)
    phase("sums0")
    slot_sums(0)
    phase("a2adown")
    terms_arrived(1)
    phase("sums1")
    slot_sums(1)
    phase("rsx0")
    x_sums(0)
    phase("rsx1")
    x_sums(1)
    phase("rsz0")
    finish(0, gu_ref)
    phase("rsz1")
    finish(1, gd_ref)
    phase("drain")
    for cp in sends:
        cp.wait_send()
    z_done()
    gz_done()
    phase(None)


def per_device(*args):
    anyspec = pl.BlockSpec(memory_space=pl.ANY)
    vm = pl.BlockSpec(memory_space=pltpu.VMEM)
    sm = pl.BlockSpec(memory_space=pltpu.SMEM)
    big = pltpu.VMEM((FT, D), BF16)
    block = lambda *lead: pltpu.VMEM((*lead, RB, LANES), BF16)
    part = lambda *lead, dtype=BF16: pltpu.VMEM((2, *lead, HALF, LANES), dtype)
    return pl.pallas_call(
        kernel,
        out_shape=(
            jax.ShapeDtypeStruct((1, RANK, RB), F32),
            jax.ShapeDtypeStruct((1, RANK, RB), F32),
            jax.ShapeDtypeStruct((1,), F32),
        ),
        in_specs=[anyspec] * 6 + [vm] * 2 + [sm] * 3,
        out_specs=(vm, vm, sm),
        scratch_shapes=[
            big, big, big, big, big,
            pltpu.VMEM((D, D), BF16),
            big,
            pltpu.VMEM((FT, D), F32),
            big,
            pltpu.VMEM((16, 8, LANES), jnp.int32),
            block(), block(16), block(16), block(16),
            part(16), part(16), part(16, dtype=F32), part(16),
            part(3, 4), part(4, dtype=F32), part(4), part(3),
            pltpu.VMEM((FT, RANK), BF16),
            pltpu.VMEM((FT, LANES), BF16),
            pltpu.VMEM((FT, RANK), BF16),
            pltpu.SMEM((16,), jnp.int32),
            pltpu.SemaphoreType.DMA((N_SEMS,)),
            pltpu.SemaphoreType.DMA((N_SEMS,)),
            pltpu.SemaphoreType.DMA((8,)),
        ],
        compiler_params=pltpu.CompilerParams(
            collective_id=0, has_side_effects=True, vmem_limit_bytes=60 * 2**20
        ),
        name="step",
    )(*args)


def solution(mesh):
    wide = P(("frame", "fsdp"), None, None)
    flat = P(("frame", "fsdp"))
    adapter = P("frame", None, "fsdp")
    return jax.shard_map(
        per_device,
        mesh=mesh,
        in_specs=(wide,) * 5 + (P("fsdp", None), adapter, adapter, flat, P(), flat),
        out_specs=(adapter, adapter, flat),
        check_vma=False,
    )
```

```python
import functools
import math

import jax
import jax.numpy as jnp
from jax import lax
from jax.experimental import pallas as pl
from jax.experimental.pallas import tpu as pltpu
from jax.sharding import PartitionSpec as P

HEADS = 24
HD = 128
FT = 192
D = 3072
RANK = 64
SC = 16
RB = D // 16
HALF = RB // 2
NB = 512
LANES = 128
K_OWN = 4
K_FAR = 4
PARTS = 4
PR = HALF // 2
RELAY = 1
FAR = PARTS
MESH = pl.DeviceIdType.MESH
F32 = jnp.float32
BF16 = jnp.bfloat16
SCALE = 1.0 / math.sqrt(HD)


def dot(a, b, ca, cb):
    return lax.dot_general(a, b, (((ca,), (cb,)), ((), ())), preferred_element_type=F32)


class Sems:
    def __init__(self, send, recv):
        self.send, self.recv, self.out, self.into = send, recv, 0, 0

    def sender(self):
        self.out += 1
        return self.out - 1

    def receiver(self):
        self.into += 1
        return self.into - 1

    def copy(self, out, into, src, dst, dev):
        return pltpu.make_async_remote_copy(
            src_ref=src, dst_ref=dst, send_sem=self.send.at[out], recv_sem=self.recv.at[into],
            device_id=dev, device_id_type=MESH,
        )


N_SEND, N_RECV = 40, 72


class Phase:
    def __init__(self):
        self.scope = None

    def __call__(self, name):
        if self.scope is not None:
            self.scope.__exit__(None, None, None)
        self.scope = None
        if name:
            self.scope = jax.named_scope(name)
            self.scope.__enter__()


def kernel(
    q_hbm, k_hbm, v_hbm, res_hbm, tgt_hbm, w_hbm, down_hbm, up_hbm, scene_ref, row_ref, count_ref,
    grad_ref, loss_ref,
    pair, q, k, v, res, tgt, w, att, acc, cot, slots, bundle, gath, picked, du, terms, got, dense, dense16,
    xgot, xsum, xsum16, zgot, zfar, lvec, lhigh, blvec, slot_sm, ssem, rsem, lsem,
):
    phase = Phase()
    phase("entry")
    sems = Sems(ssem, rsem)
    i = lax.axis_index("frame")
    j = lax.axis_index("fsdp")
    x, zl = i // 4, i % 4
    hi, y, c = j // 8, (j // 2) % 4, j % 2
    far = 1 - hi
    edge = jnp.logical_or(zl == 0, zl == 3)
    inner_zl = jnp.where(zl == 0, 1, 2)

    def fs(h, yy, cc):
        return h * 8 + yy * 2 + cc

    def at_y(dy):
        return (i, fs(hi, (y + dy + 4) % 4, c))

    def at_x(dx):
        return (((x + dx + 4) % 4) * 4 + zl, j)

    partner = (x * 4 + 3 - zl, fs(far, y, c))

    def across(zz):
        return (x * 4 + zz, fs(far, y, c))

    twin = (i, j + 1 - 2 * c)

    barrier = pltpu.get_barrier_semaphore()
    peers = [(i, (j + d) % 16) for d in range(1, 16)]
    peers += [at_x(d) for d in range(1, 4)]
    peers += [(x * 4 + (zl + d) % 4, j) for d in range(1, 4)]
    peers += [across((zl + d) % 4) for d in range(1, 4)]
    for peer in peers:
        pl.semaphore_signal(barrier, inc=1, device_id=peer, device_id_type=MESH)

    pair_loads = [
        pltpu.make_async_copy(src.at[0], pair.at[n], lsem.at[6 + n])
        for n, src in enumerate((down_hbm, up_hbm))
    ]
    for cp in pair_loads:
        cp.start()
    loads = []
    for n, (src, dst) in enumerate(((q_hbm, q), (k_hbm, k), (v_hbm, v), (res_hbm, res), (tgt_hbm, tgt))):
        cp = pltpu.make_async_copy(src.at[0], dst, lsem.at[n])
        cp.start()
        loads.append(cp)
    own_row = pl.multiple_of(j * RB, RB)
    own_load = pltpu.make_async_copy(w_hbm, w.at[pl.ds(own_row, RB)], lsem.at[5])
    own_load.start()

    phase("barrier")
    pl.semaphore_wait(barrier, len(peers))

    def quarter(cls, xx):
        kk = K_OWN if cls == 0 else K_FAR
        return pl.ds(pl.multiple_of(xx * (kk * LANES), LANES), kk * LANES)

    def rest(cls, part):
        kk = K_OWN if cls == 0 else K_FAR
        size = (D - 4 * kk * LANES) // 2
        return pl.ds(4 * kk * LANES + part * size, size)

    def shard_row(h, yy):
        return pl.multiple_of(fs(h, yy, c) * RB, RB)

    def half_rows(h, yy, s):
        return pl.ds(pl.multiple_of(shard_row(h, yy) + s * HALF, HALF), HALF)

    def push(ids, src, dst, dev):
        sems.copy(ids[0], ids[1], src, dst, dev).start()

    def arrived(ids, like):
        sems.copy(ids[0], ids[1], like, like, twin).wait_recv()

    def sent(ids, like):
        sems.copy(ids[0], ids[1], like, like, twin).wait_send()

    hs = (hi, far)
    DIRS = (1, -1)
    FIRST = (0, 1)
    PC = K_OWN * LANES

    def like(halves):
        return w.at[pl.ds(0, halves * HALF), pl.ds(0, PC)]

    y_out = [sems.sender() for _ in range(2)]
    y_id = [[[(y_out[cls], sems.receiver()) for _ in range(3)] for _ in range(3)] for cls in range(2)]
    z_id = [[(sems.sender(), sems.receiver()) for _ in range(2)] for _ in range(3)]
    shards = [(1, 0), (0, 1), (0, 3), (0, 2), (1, 1), (1, 3), (1, 2)]
    x_out = sems.sender()
    x_id = [[(x_out, sems.receiver()) for _ in range(2)] for _ in range(7)]
    die_out = sems.sender()
    die_id = [(die_out, sems.receiver()) for _ in range(8)]

    def cols_of(cls, piece):
        return quarter(cls, x) if piece == 0 else rest(cls, piece - 1)

    def y_send(cls, piece, from_hbm):
        for n in range(2):
            for dn, d in enumerate(DIRS):
                s = FIRST[dn] if n == 0 else 1 - FIRST[dn]
                cols = cols_of(cls, piece)
                dst = w.at[half_rows(hs[cls], y, s), cols]
                src = w_hbm.at[pl.ds(s * HALF, HALF), cols] if from_hbm else dst
                push(y_id[cls][piece][n], src, dst, at_y(d))

    def y_forward(cls, piece):
        arrived(y_id[cls][piece][0], like(2))
        for dn, d in enumerate(DIRS):
            reg = w.at[half_rows(hs[cls], (y - d + 4) % 4, FIRST[dn]), cols_of(cls, piece)]
            push(y_id[cls][piece][2], reg, reg, at_y(d))

    def y_second(cls, piece):
        arrived(y_id[cls][piece][1], like(2))

    def y_last(cls, piece):
        arrived(y_id[cls][piece][2], like(2))

    def x_send(n, s):
        cls, dy = shards[n]
        for dn, d in enumerate(DIRS):
            reg = w.at[half_rows(hs[cls], (y + dy) % 4, s), quarter(cls, x)]
            push(x_id[n][0 if s == FIRST[dn] else 1], reg, reg, at_x(d))

    def x_forward(n):
        cls, dy = shards[n]
        arrived(x_id[n][0], like(2))
        for dn, d in enumerate(DIRS):
            reg = w.at[half_rows(hs[cls], (y + dy) % 4, FIRST[dn]), quarter(cls, (x - d + 4) % 4)]
            push(x_id[n][1], reg, reg, at_x(d))

    def x_finish(n):
        arrived(x_id[n][1], like(4))

    def z_cols(p):
        return cols_of(1, p)

    def z_start():
        @pl.when(edge)
        def _():
            for p in range(3):
                push(z_id[p][0], w_hbm.at[:, z_cols(p)], w.at[pl.ds(own_row, RB), z_cols(p)], partner)

    far_rows = pl.ds(shard_row(far, y), RB)

    def z_edge(p):
        reg = w.at[far_rows, z_cols(p)]

        @pl.when(edge)
        def _():
            arrived(z_id[p][0], reg)
            push(z_id[p][1], reg, reg, (x * 4 + inner_zl, j))

    def z_inner(p):
        reg = w.at[far_rows, z_cols(p)]

        @pl.when(jnp.logical_not(edge))
        def _():
            arrived(z_id[p][1], reg)

    def z_done():
        @pl.when(edge)
        def _():
            for p in range(3):
                reg = w.at[far_rows, z_cols(p)]
                sent(z_id[p][0], reg)
                sent(z_id[p][1], reg)

    mul_order = [(0, 0), (0, 1), (0, 3), (0, 2), (1, 0), (1, 1), (1, 3), (1, 2)]

    cut = 4 * K_FAR * LANES
    die_cols = (pl.ds(0, cut), pl.ds(cut, D - cut))

    def die_send(m, p):
        cls, dy = mul_order[m]
        dst = w.at[pl.ds(shard_row(hs[cls], (y + dy) % 4), RB), die_cols[p]]
        src = w_hbm.at[:, die_cols[p]] if m == 0 else dst
        push(die_id[m], src, dst, twin)

    def die_take(m):
        cls, dy = mul_order[m]
        r = pl.multiple_of(fs(hs[cls], (y + dy) % 4, 1 - c) * RB, RB)
        arrived(die_id[m], w.at[pl.ds(r, RB)])

    count = count_ref[0]

    def heads(lo, up):
        def one(h, carry):
            cols = pl.ds(pl.multiple_of(h * HD, HD), HD)
            s = dot(q[:, cols], k[:, cols], 1, 1) * SCALE
            pos = lax.broadcasted_iota(jnp.int32, (FT, FT), 1)
            s = jnp.where(pos < count, s, -jnp.inf)
            e = jnp.exp(s - jnp.max(s, axis=1, keepdims=True))
            p = (e / jnp.sum(e, axis=1, keepdims=True)).astype(BF16)
            att[:, cols] = dot(p, v[:, cols], 1, 0).astype(BF16)
            return carry

        lax.fori_loop(lo, up, one, 0, unroll=2)

    def pair_row(m):
        cls, dy = mul_order[m]
        return pl.multiple_of(fs(hs[cls], (y + dy) % 4, 0) * RB, 2 * RB)

    def multiply(*group):
        def one(n, carry):
            cols = pl.ds(pl.multiple_of(n * NB, NB), NB)
            total = None if group[0] == 0 else acc[:, cols]
            for m in group:
                rows = pl.ds(pair_row(m), 2 * RB)
                part = dot(att[:, rows], w[rows, cols], 1, 0)
                total = part if total is None else total + part
            acc[:, cols] = total
            return carry

        lax.fori_loop(0, D // NB, one, 0)

    phase("start")
    z_start()
    y_send(0, 0, True)
    my_slot = row_ref[scene_ref[0]]
    slots[pl.ds(j, 1)] = jnp.full((1, 8, LANES), my_slot, jnp.int32)
    for cp in pair_loads:
        cp.wait()
    both = jnp.concatenate([pair[0].astype(F32), pair[1].astype(F32)], axis=0)
    both = jnp.concatenate([both, jnp.zeros((2 * RANK, 256 - RB), F32)], axis=1)
    bundle[...] = both.T[:RB].astype(BF16)
    gath[pl.ds(zl * 4 + x, 1)] = bundle[...][None]

    def gz_copy(dn, t):
        d = DIRS[dn]
        reg = gath.at[pl.ds((zl - d * t) * 4, 4)]
        return sems.copy(*gz_id[dn][t], reg, reg, (x * 4 + zl + d, j))

    def gz_has(dn, t):
        return zl >= t if dn == 0 else zl <= 3 - t

    def gz_goes(dn, t):
        return jnp.logical_and(gz_has(dn, t), zl < 3 if dn == 0 else zl > 0)

    def gz_hop(t):
        for dn in range(2):
            @pl.when(gz_goes(dn, t))
            def _():
                gz_copy(dn, t).start()

    def gz_take(t):
        for dn in range(2):
            @pl.when(gz_has(dn, t + 1))
            def _():
                reg = gath.at[pl.ds((zl - DIRS[dn] * (t + 1)) * 4, 4)]
                arrived(gz_id[dn][t], reg)

    def gz_done():
        for t in range(3):
            for dn in range(2):
                @pl.when(gz_goes(dn, t))
                def _():
                    gz_copy(dn, t).wait_send()

    gz_id = [[(sems.sender(), sems.receiver()) for _ in range(3)] for _ in range(2)]

    def both_ids():
        return sems.sender(), sems.receiver()

    slot_id, gx_id, pick_id, zfar_id = (both_ids() for _ in range(4))
    term_id = [both_ids() for _ in range(PARTS)]
    rx_id = [both_ids() for _ in range(PARTS + 1)]
    rz_id = [both_ids() for _ in range(PARTS)]
    for d in (2, 1, 3):
        push(gx_id, bundle, gath.at[zl * 4 + x], at_x(d))
    for d in range(1, 16):
        push(slot_id, slots.at[j], slots.at[j], (i, (j + d) % 16))
    y_send(0, 1, True)
    die_send(0, 0)
    die_send(0, 1)

    phase("h0_6")
    for cp in loads[:3]:
        cp.wait()
    heads(0, 6)
    phase("yf00")
    y_forward(0, 0)
    x_send(2, 0)
    x_send(1, 1)
    y_second(0, 0)
    x_send(2, 1)
    x_send(1, 0)
    phase("ze0")
    z_edge(0)
    arrived(gx_id, gath.at[pl.ds(0, 3)])
    gz_hop(0)
    phase("h6_12")
    heads(6, 12)
    phase("zi0")
    z_inner(0)
    y_send(1, 0, False)
    x_send(0, 0)
    x_send(0, 1)
    y_send(0, 2, True)
    phase("yl00")
    y_last(0, 0)
    x_send(3, 0)
    x_send(3, 1)
    phase("yf01")
    y_forward(0, 1)
    phase("ze1")
    z_edge(1)
    gz_take(0)
    gz_hop(1)
    phase("h12_16")
    heads(12, 16)
    phase("xf21")
    x_forward(2)
    x_forward(1)
    phase("yf10")
    y_forward(1, 0)
    x_send(5, 0)
    x_send(4, 1)
    y_second(1, 0)
    x_send(5, 1)
    x_send(4, 0)
    phase("ze2")
    z_edge(2)
    gz_take(1)
    gz_hop(2)
    phase("h16_20")
    heads(16, 20)
    phase("zi1")
    z_inner(1)
    y_send(1, 1, False)
    phase("xf0")
    x_forward(0)
    phase("h20_24")
    heads(20, 24)
    phase("xf3")
    x_forward(3)
    phase("yf02")
    y_forward(0, 2)
    phase("zi2")
    z_inner(2)
    y_send(1, 2, False)
    phase("slotgz")
    arrived(slot_id, slots.at[pl.ds(0, 15)])
    gz_take(2)
    phase("pick")
    for f in range(16):
        slot_sm[f] = jnp.max(slots[f])
    for f in range(16):
        picked[f] = gath[(slot_sm[f] % 4) * 4 + slot_sm[f] // 4]
    for d in (8, 7, 9, 6, 10, 5, 11, 4, 12, 3, 13, 2, 14, 1, 15):
        to = (j + d) % 16
        push(pick_id, picked.at[to], du.at[j], (i, to))
    du[pl.ds(j, 1)] = picked[pl.ds(j, 1)]
    phase("yl10")
    y_last(1, 0)
    x_send(6, 0)
    x_send(6, 1)
    phase("mul0")
    own_load.wait()
    die_take(0)
    multiply(0)
    phase("yf11")
    y_forward(1, 1)
    phase("fin12")
    y_second(0, 1)
    y_second(0, 2)
    die_send(1, 1)
    die_send(2, 1)
    x_finish(2)
    x_finish(1)
    die_send(1, 0)
    die_send(2, 0)
    phase("xf54")
    x_forward(5)
    x_forward(4)
    phase("mul12")
    die_take(1)
    die_take(2)
    multiply(1, 2)
    phase("fin34")
    y_last(0, 1)
    y_last(0, 2)
    die_send(3, 1)
    die_send(4, 1)
    x_finish(0)
    die_send(4, 0)
    x_finish(3)
    die_send(3, 0)
    phase("yf12")
    y_forward(1, 2)
    phase("xf6")
    x_forward(6)
    phase("mul34")
    die_take(3)
    die_take(4)
    multiply(3, 4)
    phase("ys1")
    y_second(1, 1)
    y_second(1, 2)
    die_send(5, 1)
    die_send(6, 1)
    phase("xfin54")
    x_finish(5)
    die_send(6, 0)
    x_finish(4)
    die_send(5, 0)
    phase("pickwait")
    arrived(pick_id, du.at[pl.ds(0, 15)])
    phase("low")
    lane = lax.broadcasted_iota(jnp.int32, (FT, LANES), 1)

    def low(n, total):
        return total + dot(
            att[:, pl.ds(pl.multiple_of(n * 384, 384), 384)],
            du[pl.ds(n * 2, 2)].reshape(384, LANES), 1, 0,
        )

    lr = lax.fori_loop(0, 8, low, jnp.zeros((FT, LANES), F32), unroll=4).astype(BF16).astype(F32)
    lr = jnp.where(lane < RANK, 2.0 * lr, 0.0)
    lvec[...] = lr[:, :RANK].astype(BF16)
    lhigh[...] = pltpu.roll(lr, RANK, 1).astype(BF16)
    for cp in loads[3:]:
        cp.wait()
    row = lax.broadcasted_iota(jnp.int32, (FT, 1), 0)
    valid = row < count
    phase("yl1")
    y_last(1, 1)
    y_last(1, 2)
    die_send(7, 1)
    phase("fin7")
    x_finish(6)
    die_send(7, 0)
    phase("die56")
    die_take(5)
    die_take(6)
    phase("die7")
    die_take(7)
    phase("back")
    inv = 2.0 / count.astype(F32)
    ND = 2 * RB
    chip = j // 2
    half_lane = lax.broadcasted_iota(jnp.int32, (32, LANES), 1) < 64
    late = [pl.ds(pair_row(m), 2 * RB) for m in (5, 6, 7)]

    def pack(h, n, t):
        top, bottom = t[:32, 128:256], t[32:, 128:256]
        packs = (
            (t[:, :128], jnp.where(half_lane, top, pltpu.roll(bottom, 64, 1))),
            (t[:, 256:], jnp.where(half_lane, pltpu.roll(top, 64, 1), bottom)),
        )
        for b in range(2):
            at = pl.ds(n * 2 + b, 1)
            whole, thin = packs[b]
            terms[2 * h, at] = whole[:PR].astype(BF16)[None]
            terms[2 * h + 1, at, : 64 - PR] = whole[PR:].astype(BF16)[None]
            terms[2 * h + 1, at, 64 - PR :] = thin.astype(BF16)[None]

    STEPS = (4, 3, 5, 2, 6, 1, 7, 0)

    def ship_part(h, step):
        n = (chip + step) % 8
        for rel in range(2):
            b = (c + rel) % 2
            block = n * 2 + b
            if h != RELAY:
                to, at = block, j
            else:
                to = hi * 8 + (n % 4) * 2 + b
                at = j % 8 + 8 * far_block(n)
            if rel == 0 and step % (8 if h != RELAY else 4) == 0:
                got[h, pl.ds(at, 1)] = terms[h, pl.ds(block, 1)]
            else:
                push(term_id[h], terms.at[h, block], got.at[h, at], (i, to))

    def far_block(n):
        return jnp.where(n // 4 == hi, 0, 1)

    def terms_arrived(h):
        arrived(term_id[h], got.at[h, pl.ds(0, 14 if h == RELAY else 15)])

    loss = jnp.zeros((8, ND), F32)
    bl = jnp.zeros((FT, LANES), F32)
    for step in STEPS:
        n = (chip + step) % 8
        cols = pl.ds(pl.multiple_of(n * ND, ND), ND)
        dn_ = du[pl.ds(n * 2, 2)].reshape(ND, LANES)
        e = acc[:, cols] + dot(lhigh[...], dn_, 1, 1)
        for rows in late:
            e = e + dot(att[:, rows], w[rows, cols], 1, 0)
        e = e + res[:, cols].astype(F32) - tgt[:, cols].astype(F32)
        e = jnp.where(valid, e, 0.0)
        loss = loss + jnp.sum((e * e).reshape(FT // 8, 8, ND), axis=0)
        ct = (inv * e).astype(BF16)
        bl = bl + dot(ct, dn_, 1, 0)
        pack(0, n, dot(lvec[...], ct, 0, 0))
        ship_part(1, step)
        ship_part(0, step)
    phase("down")
    blvec[...] = pltpu.roll(2.0 * bl, RANK, 1)[:, :RANK].astype(BF16)
    for step in STEPS:
        n = (chip + step) % 8
        cols = pl.ds(pl.multiple_of(n * ND, ND), ND)
        pack(1, n, dot(blvec[...], att[:, cols], 0, 0))
        ship_part(2, step)
    for step in STEPS:
        ship_part(3, step)
    loss_ref[0] = jnp.sum(loss) / (count.astype(F32) * D)

    def slot_sums(h):
        runs = ((h, 0, 0, 16),) if h != RELAY else ((h, 0, hi * 8, 8), (FAR, 8, hi * 8, 8))

        def one(n, carry):
            rows = pl.ds(pl.multiple_of(n * 16, 16), 16)
            for stream, first, frame, many in runs:
                parts = [got[h, first + f, rows].astype(F32) for f in range(many)]
                for s in range(SC):
                    total = jnp.zeros((16, LANES), F32)
                    for f in range(many):
                        total = total + jnp.where(slot_sm[frame + f] == s, 1.0, 0.0) * parts[f]
                    dense[stream, s, rows] = total
                    dense16[stream, s, rows] = total.astype(BF16)
            return carry

        lax.fori_loop(0, PR // 16, one, 0)
        for stream, *_ in runs:
            for d in (2, 1, 3):
                to = (x + d) % 4
                push(rx_id[stream], dense16.at[stream, pl.ds(to * 4, 4)], xgot.at[stream, d - 1], at_x(d))

    def x_sums(h):
        for stream in (h,) if h != RELAY else (h, FAR):
            arrived(rx_id[stream], xgot.at[stream])
            for s in range(4):
                total = dense[stream, pl.ds(x * 4 + s, 1)][0]
                for d in range(3):
                    total = total + xgot[stream, d, s].astype(F32)
                if stream != FAR:
                    xsum[stream, s] = total
                xsum16[stream, s] = total.astype(BF16)
            if stream == FAR:
                for s in range(4):
                    push(zfar_id, xsum16.at[stream, s], zfar.at[zl], across(s))
            else:
                for d in range(1, 4):
                    to = (zl + d) % 4
                    push(rz_id[stream], xsum16.at[stream, to], zgot.at[stream, d - 1], (x * 4 + to, j))

    def finish(h):
        arrived(rz_id[h], zgot.at[h])
        total = xsum[h, pl.ds(zl, 1)][0]
        for d in range(3):
            total = total + zgot[h, d].astype(F32)
        if h == RELAY:
            arrived(zfar_id, zfar)
            for d in range(4):
                total = total + zfar[d].astype(F32)
        return total

    def unpack(first, second):
        wide = jnp.concatenate([first, second[: 64 - PR]], axis=0)
        thin = second[64 - PR :]
        thin = jnp.concatenate([thin, pltpu.roll(thin, 64, 1)], axis=0)
        turned = pltpu.roll(wide, 64, 1)
        lanes = lax.broadcasted_iota(jnp.int32, (64, LANES), 1)
        even = jnp.concatenate([wide, thin], axis=1)
        odd = jnp.concatenate([jnp.where(lanes < 64, thin, turned), turned], axis=1)
        return jnp.where(c == 0, even, odd)[:, :RB]

    def turn(h, before):
        phase(f"a2a{h}")
        terms_arrived(h)
        phase(f"sums{h}")
        slot_sums(h)
        if before is not None:
            phase(f"rsx{before}")
            x_sums(before)

    turn(1, None)
    turn(0, 1)
    turn(2, 0)
    turn(3, 2)
    phase("rsz01")
    grad_ref[1] = unpack(finish(0), finish(1))
    phase("rsx3")
    x_sums(3)
    phase("rsz23")
    grad_ref[0] = unpack(finish(2), finish(3))
    phase("drain")
    for cls in range(2):
        sent(y_id[cls][0][0], like(18))
    sent(x_id[0][0], w.at[pl.ds(0, 21 * HALF), pl.ds(0, 2 * PC)])
    sent(die_id[0], w.at[pl.ds(0, 8 * RB)])
    sent(slot_id, slots.at[pl.ds(0, 15)])
    sent(gx_id, gath.at[pl.ds(0, 3)])
    sent(pick_id, picked.at[pl.ds(0, 15)])
    for h in range(PARTS):
        sent(term_id[h], terms.at[h, pl.ds(0, 14 if h == RELAY else 15)])
        sent(rz_id[h], zgot.at[h])
    for stream in range(PARTS + 1):
        sent(rx_id[stream], xgot.at[stream])
    sent(zfar_id, zfar)
    z_done()
    gz_done()
    phase(None)


def per_device(*args):
    anyspec = pl.BlockSpec(memory_space=pl.ANY)
    vm = pl.BlockSpec(memory_space=pltpu.VMEM)
    sm = pl.BlockSpec(memory_space=pltpu.SMEM)
    big = pltpu.VMEM((FT, D), BF16)
    block = lambda *lead: pltpu.VMEM((*lead, RB, LANES), BF16)
    stream = lambda *lead, dtype=BF16: pltpu.VMEM((PARTS + 1, *lead, PR, LANES), dtype)
    part = lambda *lead, dtype=BF16: pltpu.VMEM((PARTS, *lead, PR, LANES), dtype)
    grads, loss = pl.pallas_call(
        kernel,
        out_shape=(
            jax.ShapeDtypeStruct((2, RANK, RB), F32),
            jax.ShapeDtypeStruct((1,), F32),
        ),
        in_specs=[anyspec] * 8 + [sm] * 3,
        out_specs=(vm, sm),
        scratch_shapes=[
            pltpu.VMEM((2, RANK, RB), BF16),
            big, big, big, big, big,
            pltpu.VMEM((D, D), BF16),
            big,
            pltpu.VMEM((FT, D), F32),
            big,
            pltpu.VMEM((16, 8, LANES), jnp.int32),
            block(), block(16), block(16), block(16),
            part(16), part(16), stream(16, dtype=F32), stream(16),
            stream(3, 4), part(4, dtype=F32), stream(4), part(3),
            pltpu.VMEM((4, PR, LANES), BF16),
            pltpu.VMEM((FT, RANK), BF16),
            pltpu.VMEM((FT, LANES), BF16),
            pltpu.VMEM((FT, RANK), BF16),
            pltpu.SMEM((16,), jnp.int32),
            pltpu.SemaphoreType.DMA((N_SEND,)),
            pltpu.SemaphoreType.DMA((N_RECV,)),
            pltpu.SemaphoreType.DMA((8,)),
        ],
        compiler_params=pltpu.CompilerParams(
            collective_id=0, has_side_effects=True, vmem_limit_bytes=60 * 2**20
        ),
        name="step",
    )(*args)
    return grads[:1], grads[1:], loss


def solution(mesh):
    wide = P(("frame", "fsdp"), None, None)
    flat = P(("frame", "fsdp"))
    adapter = P("frame", None, "fsdp")
    return jax.shard_map(
        per_device,
        mesh=mesh,
        in_specs=(wide,) * 5 + (P("fsdp", None), adapter, adapter, flat, P(), flat),
        out_specs=(adapter, adapter, flat),
        check_vma=False,
    )
```

```python
import functools
import math

import jax
import jax.numpy as jnp
from jax import lax
from jax.experimental import pallas as pl
from jax.experimental.pallas import tpu as pltpu
from jax.sharding import PartitionSpec as P

HEADS = 24
HD = 128
FT = 192
D = 3072
RANK = 64
SC = 16
RB = D // 16
HALF = RB // 2
NB = 512
LANES = 128
K_OWN = 4
K_FAR = 4
PARTS = 5
PR = (48, 48, 48, 32, 16)
PMAX = 48
RELAY = 1
FAR = PARTS
SR = PR + (PR[RELAY],)
MESH = pl.DeviceIdType.MESH
F32 = jnp.float32
BF16 = jnp.bfloat16
SCALE = 1.0 / math.sqrt(HD)


def dot(a, b, ca, cb):
    return lax.dot_general(a, b, (((ca,), (cb,)), ((), ())), preferred_element_type=F32)


class Sems:
    def __init__(self, send, recv):
        self.send, self.recv, self.out, self.into = send, recv, 0, 0

    def sender(self):
        self.out += 1
        return self.out - 1

    def receiver(self):
        self.into += 1
        return self.into - 1

    def copy(self, out, into, src, dst, dev):
        return pltpu.make_async_remote_copy(
            src_ref=src, dst_ref=dst, send_sem=self.send.at[out], recv_sem=self.recv.at[into],
            device_id=dev, device_id_type=MESH,
        )


N_SEND, N_RECV = 40, 72


class Phase:
    def __init__(self):
        self.scope = None

    def __call__(self, name):
        if self.scope is not None:
            self.scope.__exit__(None, None, None)
        self.scope = None
        if name:
            self.scope = jax.named_scope(name)
            self.scope.__enter__()


def kernel(
    q_hbm, k_hbm, v_hbm, res_hbm, tgt_hbm, w_hbm, down_hbm, up_hbm, scene_hbm, row_hbm, count_hbm,
    grad_ref, loss_ref,
    scene_ref, row_ref, count_ref, pair, q, k, v, res, tgt, w, att, acc, cot, slots, bundle, gath, picked, du, terms, got, dense, dense16,
    xgot, xsum, xsum16, zgot, zfar, lvec, lhigh, blvec, slot_sm, ssem, rsem, lsem,
):
    phase = Phase()
    phase("entry")
    sems = Sems(ssem, rsem)
    i = lax.axis_index("frame")
    j = lax.axis_index("fsdp")
    x, zl = i // 4, i % 4
    hi, y, c = j // 8, (j // 2) % 4, j % 2
    far = 1 - hi
    edge = jnp.logical_or(zl == 0, zl == 3)
    inner_zl = jnp.where(zl == 0, 1, 2)

    def fs(h, yy, cc):
        return h * 8 + yy * 2 + cc

    def at_y(dy):
        return (i, fs(hi, (y + dy + 4) % 4, c))

    def at_x(dx):
        return (((x + dx + 4) % 4) * 4 + zl, j)

    partner = (x * 4 + 3 - zl, fs(far, y, c))

    def across(zz):
        return (x * 4 + zz, fs(far, y, c))

    twin = (i, j + 1 - 2 * c)

    barrier = pltpu.get_barrier_semaphore()
    peers = [(i, (j + d) % 16) for d in range(1, 16)]
    peers += [at_x(d) for d in range(1, 4)]
    peers += [(x * 4 + (zl + d) % 4, j) for d in range(1, 4)]
    peers += [across((zl + d) % 4) for d in range(1, 4)]
    for peer in peers:
        pl.semaphore_signal(barrier, inc=1, device_id=peer, device_id_type=MESH)

    pair_loads = [
        pltpu.make_async_copy(src.at[0], pair.at[n], lsem.at[6 + n])
        for n, src in enumerate((down_hbm, up_hbm))
    ]
    pair_loads += [
        pltpu.make_async_copy(src, dst, lsem.at[8 + n])
        for n, (src, dst) in enumerate(
            ((scene_hbm, scene_ref), (row_hbm, row_ref), (count_hbm, count_ref))
        )
    ]
    for cp in pair_loads:
        cp.start()
    loads = []
    for n, (src, dst) in enumerate(((q_hbm, q), (k_hbm, k), (v_hbm, v), (res_hbm, res), (tgt_hbm, tgt))):
        cp = pltpu.make_async_copy(src.at[0], dst, lsem.at[n])
        cp.start()
        loads.append(cp)
    own_row = pl.multiple_of(j * RB, RB)
    own_load = pltpu.make_async_copy(w_hbm, w.at[pl.ds(own_row, RB)], lsem.at[5])
    own_load.start()

    phase("barrier")
    pl.semaphore_wait(barrier, len(peers))

    def quarter(cls, xx):
        kk = K_OWN if cls == 0 else K_FAR
        return pl.ds(pl.multiple_of(xx * (kk * LANES), LANES), kk * LANES)

    def rest(cls, part):
        kk = K_OWN if cls == 0 else K_FAR
        size = (D - 4 * kk * LANES) // 2
        return pl.ds(4 * kk * LANES + part * size, size)

    def shard_row(h, yy):
        return pl.multiple_of(fs(h, yy, c) * RB, RB)

    def half_rows(h, yy, s):
        return pl.ds(pl.multiple_of(shard_row(h, yy) + s * HALF, HALF), HALF)

    def push(ids, src, dst, dev):
        sems.copy(ids[0], ids[1], src, dst, dev).start()

    def arrived(ids, like):
        sems.copy(ids[0], ids[1], like, like, twin).wait_recv()

    def sent(ids, like):
        sems.copy(ids[0], ids[1], like, like, twin).wait_send()

    hs = (hi, far)
    DIRS = (1, -1)
    FIRST = (0, 1)
    PC = K_OWN * LANES

    def like(halves):
        return w.at[pl.ds(0, halves * HALF), pl.ds(0, PC)]

    y_out = [sems.sender() for _ in range(2)]
    y_id = [[[(y_out[cls], sems.receiver()) for _ in range(3)] for _ in range(3)] for cls in range(2)]
    z_id = [[(sems.sender(), sems.receiver()) for _ in range(2)] for _ in range(3)]
    shards = [(1, 0), (0, 1), (0, 3), (0, 2), (1, 1), (1, 3), (1, 2)]
    x_out = sems.sender()
    x_id = [[(x_out, sems.receiver()) for _ in range(2)] for _ in range(7)]
    die_out = sems.sender()
    die_id = [(die_out, sems.receiver()) for _ in range(8)]

    def cols_of(cls, piece):
        return quarter(cls, x) if piece == 0 else rest(cls, piece - 1)

    def y_send(cls, piece, from_hbm):
        for n in range(2):
            for dn, d in enumerate(DIRS):
                s = FIRST[dn] if n == 0 else 1 - FIRST[dn]
                cols = cols_of(cls, piece)
                dst = w.at[half_rows(hs[cls], y, s), cols]
                src = w_hbm.at[pl.ds(s * HALF, HALF), cols] if from_hbm else dst
                push(y_id[cls][piece][n], src, dst, at_y(d))

    def y_forward(cls, piece):
        arrived(y_id[cls][piece][0], like(2))
        for dn, d in enumerate(DIRS):
            reg = w.at[half_rows(hs[cls], (y - d + 4) % 4, FIRST[dn]), cols_of(cls, piece)]
            push(y_id[cls][piece][2], reg, reg, at_y(d))

    def y_second(cls, piece):
        arrived(y_id[cls][piece][1], like(2))

    def y_last(cls, piece):
        arrived(y_id[cls][piece][2], like(2))

    def x_send(n, s):
        cls, dy = shards[n]
        for dn, d in enumerate(DIRS):
            reg = w.at[half_rows(hs[cls], (y + dy) % 4, s), quarter(cls, x)]
            push(x_id[n][0 if s == FIRST[dn] else 1], reg, reg, at_x(d))

    def x_forward(n):
        cls, dy = shards[n]
        arrived(x_id[n][0], like(2))
        for dn, d in enumerate(DIRS):
            reg = w.at[half_rows(hs[cls], (y + dy) % 4, FIRST[dn]), quarter(cls, (x - d + 4) % 4)]
            push(x_id[n][1], reg, reg, at_x(d))

    def x_finish(n):
        arrived(x_id[n][1], like(4))

    def z_cols(p):
        return cols_of(1, p)

    def z_start():
        @pl.when(edge)
        def _():
            for p in range(3):
                push(z_id[p][0], w_hbm.at[:, z_cols(p)], w.at[pl.ds(own_row, RB), z_cols(p)], partner)

    far_rows = pl.ds(shard_row(far, y), RB)

    def z_edge(p):
        reg = w.at[far_rows, z_cols(p)]

        @pl.when(edge)
        def _():
            arrived(z_id[p][0], reg)
            push(z_id[p][1], reg, reg, (x * 4 + inner_zl, j))

    def z_inner(p):
        reg = w.at[far_rows, z_cols(p)]

        @pl.when(jnp.logical_not(edge))
        def _():
            arrived(z_id[p][1], reg)

    def z_done():
        @pl.when(edge)
        def _():
            for p in range(3):
                reg = w.at[far_rows, z_cols(p)]
                sent(z_id[p][0], reg)
                sent(z_id[p][1], reg)

    mul_order = [(0, 0), (0, 1), (0, 3), (0, 2), (1, 0), (1, 1), (1, 3), (1, 2)]

    def die_send(m, p):
        cls, dy = mul_order[m]
        rows = pl.ds(shard_row(hs[cls], (y + dy) % 4), RB)
        if p == 0:
            cols = [quarter(cls, (x + d) % 4) for d in (1, 3, 2)]
        else:
            cols = [pl.ds(4 * PC, D - 4 * PC) if p == 1 else quarter(cls, x)]
        for at in cols:
            push(die_id[m], w.at[rows, at], w.at[rows, at], twin)

    def die_own():
        rows = pl.ds(own_row, RB)
        push(die_id[0], w_hbm, w.at[rows], twin)

    def die_take(m):
        cls, dy = mul_order[m]
        r = pl.multiple_of(fs(hs[cls], (y + dy) % 4, 1 - c) * RB, RB)
        arrived(die_id[m], w.at[pl.ds(r, RB)])


    def heads(lo, up):
        def one(h, carry):
            cols = pl.ds(pl.multiple_of(h * HD, HD), HD)
            s = dot(q[:, cols], k[:, cols], 1, 1) * SCALE
            pos = lax.broadcasted_iota(jnp.int32, (FT, FT), 1)
            s = jnp.where(pos < count_ref[0], s, -jnp.inf)
            e = jnp.exp(s - jnp.max(s, axis=1, keepdims=True))
            p = (e / jnp.sum(e, axis=1, keepdims=True)).astype(BF16)
            att[:, cols] = dot(p, v[:, cols], 1, 0).astype(BF16)
            return carry

        lax.fori_loop(lo, up, one, 0, unroll=2)

    def rows_of(h):
        return pl.ds(pl.multiple_of(h * (D // 2), D // 2), D // 2)

    def multiply_own():
        def one(n, carry):
            cols = pl.ds(pl.multiple_of(n * NB, NB), NB)
            acc[:, cols] = dot(att[:, rows_of(hi)], w[rows_of(hi), cols], 1, 0)
            return carry

        lax.fori_loop(0, D // NB, one, 0)

    phase("start")
    z_start()
    y_send(0, 0, True)
    for cp in pair_loads:
        cp.wait()
    my_slot = row_ref[scene_ref[0]]
    slots[pl.ds(j, 1)] = jnp.full((1, 8, LANES), my_slot, jnp.int32)
    both = jnp.concatenate([pair[0].astype(F32), pair[1].astype(F32)], axis=0)
    both = jnp.concatenate([both, jnp.zeros((2 * RANK, 256 - RB), F32)], axis=1)
    bundle[...] = both.T[:RB].astype(BF16)
    gath[pl.ds(zl * 4 + x, 1)] = bundle[...][None]

    def gz_copy(dn, t):
        d = DIRS[dn]
        reg = gath.at[pl.ds((zl - d * t) * 4, 4)]
        return sems.copy(*gz_id[dn][t], reg, reg, (x * 4 + zl + d, j))

    def gz_has(dn, t):
        return zl >= t if dn == 0 else zl <= 3 - t

    def gz_goes(dn, t):
        return jnp.logical_and(gz_has(dn, t), zl < 3 if dn == 0 else zl > 0)

    def gz_hop(t):
        for dn in range(2):
            @pl.when(gz_goes(dn, t))
            def _():
                gz_copy(dn, t).start()

    def gz_take(t):
        for dn in range(2):
            @pl.when(gz_has(dn, t + 1))
            def _():
                reg = gath.at[pl.ds((zl - DIRS[dn] * (t + 1)) * 4, 4)]
                arrived(gz_id[dn][t], reg)

    def gz_done():
        for t in range(3):
            for dn in range(2):
                @pl.when(gz_goes(dn, t))
                def _():
                    gz_copy(dn, t).wait_send()

    gz_id = [[(sems.sender(), sems.receiver()) for _ in range(3)] for _ in range(2)]

    def both_ids():
        return sems.sender(), sems.receiver()

    slot_id, gx_id, pick_id, zfar_id = (both_ids() for _ in range(4))
    term_id = [both_ids() for _ in range(PARTS)]
    rx_id = [both_ids() for _ in range(PARTS + 1)]
    rz_id = [both_ids() for _ in range(PARTS)]
    for d in (2, 1, 3):
        push(gx_id, bundle, gath.at[zl * 4 + x], at_x(d))
    for d in range(1, 16):
        push(slot_id, slots.at[j], slots.at[j], (i, (j + d) % 16))

    phase("h0_6")
    for cp in loads[:3]:
        cp.wait()
    heads(0, 6)
    phase("yf00")
    y_forward(0, 0)
    x_send(2, 0)
    x_send(1, 1)
    y_send(0, 1, True)
    y_second(0, 0)
    x_send(2, 1)
    x_send(1, 0)
    phase("ze0")
    die_own()
    die_send(1, 2)
    die_send(2, 2)
    z_edge(0)
    arrived(gx_id, gath.at[pl.ds(0, 3)])
    gz_hop(0)
    phase("h6_12")
    heads(6, 12)
    phase("zi0")
    z_inner(0)
    y_send(1, 0, False)
    x_send(0, 0)
    x_send(0, 1)
    die_send(4, 2)
    y_send(0, 2, True)
    phase("yl00")
    y_last(0, 0)
    x_send(3, 0)
    x_send(3, 1)
    die_send(3, 2)
    phase("yf01")
    y_forward(0, 1)
    phase("ze1")
    z_edge(1)
    gz_take(0)
    gz_hop(1)
    phase("h12_16")
    heads(12, 16)
    phase("xf21")
    x_forward(2)
    x_forward(1)
    phase("yf10")
    y_forward(1, 0)
    x_send(5, 0)
    x_send(4, 1)
    y_second(1, 0)
    x_send(5, 1)
    x_send(4, 0)
    die_send(5, 2)
    die_send(6, 2)
    phase("ze2")
    z_edge(2)
    gz_take(1)
    gz_hop(2)
    phase("h16_20")
    heads(16, 20)
    phase("zi1")
    z_inner(1)
    y_send(1, 1, False)
    phase("xf0")
    x_forward(0)
    phase("h20_24")
    heads(20, 24)
    phase("xf3")
    x_forward(3)
    phase("yf02")
    y_forward(0, 2)
    phase("zi2")
    z_inner(2)
    y_send(1, 2, False)
    phase("slotgz")
    arrived(slot_id, slots.at[pl.ds(0, 15)])
    gz_take(2)
    phase("pick")
    for f in range(16):
        slot_sm[f] = jnp.max(slots[f])
    for f in range(16):
        picked[f] = gath[(slot_sm[f] % 4) * 4 + slot_sm[f] // 4]
    for d in (8, 7, 9, 6, 10, 5, 11, 4, 12, 3, 13, 2, 14, 1, 15):
        to = (j + d) % 16
        push(pick_id, picked.at[to], du.at[j], (i, to))
    du[pl.ds(j, 1)] = picked[pl.ds(j, 1)]
    phase("yl10")
    y_last(1, 0)
    x_send(6, 0)
    x_send(6, 1)
    die_send(7, 2)
    phase("yf11")
    y_forward(1, 1)
    phase("fin12")
    y_second(0, 1)
    y_second(0, 2)
    die_send(1, 1)
    die_send(2, 1)
    x_finish(2)
    x_finish(1)
    die_send(1, 0)
    die_send(2, 0)
    phase("xf54")
    x_forward(5)
    x_forward(4)
    phase("fin34")
    y_last(0, 1)
    y_last(0, 2)
    die_send(3, 1)
    die_send(4, 1)
    x_finish(0)
    die_send(4, 0)
    x_finish(3)
    die_send(3, 0)
    phase("yf12")
    y_forward(1, 2)
    phase("xf6")
    x_forward(6)
    phase("ys1")
    y_second(1, 1)
    y_second(1, 2)
    die_send(5, 1)
    die_send(6, 1)
    phase("mulown")
    own_load.wait()
    for m in range(4):
        die_take(m)
    multiply_own()
    phase("yl1")
    y_last(1, 1)
    y_last(1, 2)
    die_send(7, 1)
    phase("xfin54")
    x_finish(5)
    die_send(6, 0)
    x_finish(4)
    die_send(5, 0)
    phase("pickwait")
    arrived(pick_id, du.at[pl.ds(0, 15)])
    phase("low")
    lane = lax.broadcasted_iota(jnp.int32, (FT, LANES), 1)

    def low(n, total):
        return total + dot(
            att[:, pl.ds(pl.multiple_of(n * 384, 384), 384)],
            du[pl.ds(n * 2, 2)].reshape(384, LANES), 1, 0,
        )

    lr = lax.fori_loop(0, 8, low, jnp.zeros((FT, LANES), F32), unroll=4).astype(BF16).astype(F32)
    lr = jnp.where(lane < RANK, 2.0 * lr, 0.0)
    lvec[...] = lr[:, :RANK].astype(BF16)
    lhigh[...] = pltpu.roll(lr, RANK, 1).astype(BF16)
    for cp in loads[3:]:
        cp.wait()
    count = count_ref[0]
    row = lax.broadcasted_iota(jnp.int32, (FT, 1), 0)
    valid = row < count
    phase("fin7")
    x_finish(6)
    die_send(7, 0)
    phase("pre")

    def before(n, carry):
        cols = pl.ds(pl.multiple_of(n * 384, 384), 384)
        low_up = dot(lhigh[...], du[pl.ds(n * 2, 2)].reshape(384, LANES), 1, 1)
        acc[:, cols] = acc[:, cols] + low_up + (res[:, cols].astype(F32) - tgt[:, cols].astype(F32))
        return carry

    lax.fori_loop(0, 8, before, 0, unroll=2)
    phase("die456")
    die_take(4)
    die_take(5)
    die_take(6)
    phase("die7")
    die_take(7)
    phase("back")
    inv = 2.0 / count.astype(F32)
    ND = 4 * RB
    chip = j // 2
    half_lane = lax.broadcasted_iota(jnp.int32, (32, LANES), 1) < 64

    def pack(h, n, t):
        top, bottom = t[:32, 128:256], t[32:, 128:256]
        packs = (
            (t[:, :128], jnp.where(half_lane, top, pltpu.roll(bottom, 64, 1))),
            (t[:, 256:], jnp.where(half_lane, pltpu.roll(top, 64, 1), bottom)),
        )
        for b in range(2):
            at = pl.ds(n * 2 + b, 1)
            whole, thin = packs[b]
            whole, thin = whole.astype(BF16)[None], thin.astype(BF16)[None]
            if h == 0:
                terms[1, at] = whole[:, :48]
                terms[0, at, :16] = whole[:, 48:]
                terms[0, at, 16:] = thin
            else:
                terms[2, at] = whole[:, :48]
                terms[3, at, :16] = whole[:, 48:]
                terms[3, at, 16:32] = thin[:, :16]
                terms[4, at, :16] = thin[:, 16:]

    STEPS = (2, 1, 3, 0)

    def pair_of(step):
        return (chip // 2 + step) % 4

    def ship_part(h, step):
        for turn in range(2):
            n = pair_of(step) * 2 + (chip + turn) % 2
            for rel in range(2):
                b = (c + rel) % 2
                block = n * 2 + b
                if h != RELAY:
                    to, at = block, j
                else:
                    to = hi * 8 + (n % 4) * 2 + b
                    at = j % 8 + 8 * far_block(n)
                size = pl.ds(0, PR[h])
                if turn == 0 and rel == 0 and step % (4 if h != RELAY else 2) == 0:
                    got[h, pl.ds(at, 1), size] = terms[h, pl.ds(block, 1), size]
                else:
                    push(term_id[h], terms.at[h, block, size], got.at[h, at, size], (i, to))

    def far_block(n):
        return jnp.where(n // 4 == hi, 0, 1)

    def terms_arrived(h):
        arrived(term_id[h], got.at[h, pl.ds(0, 14 if h == RELAY else 15), pl.ds(0, PR[h])])

    loss = jnp.zeros((8, ND), F32)
    bl = jnp.zeros((FT, LANES), F32)
    for step in STEPS:
        pair_n = pair_of(step)
        cols = pl.ds(pl.multiple_of(pair_n * ND, ND), ND)
        e = acc[:, cols] + dot(att[:, rows_of(far)], w[rows_of(far), cols], 1, 0)
        e = jnp.where(valid, e, 0.0)
        loss = loss + jnp.sum((e * e).reshape(FT // 8, 8, ND), axis=0)
        ct = (inv * e).astype(BF16)
        bl = bl + dot(ct, du[pl.ds(pair_n * 4, 4)].reshape(ND, LANES), 1, 0)
        t = dot(lvec[...], ct, 0, 0)
        for n in range(2):
            pack(0, pair_n * 2 + n, t[:, n * 384 : n * 384 + 384])
        ship_part(1, step)
        ship_part(0, step)
    phase("down")
    blvec[...] = pltpu.roll(2.0 * bl, RANK, 1)[:, :RANK].astype(BF16)
    for step in STEPS:
        pair_n = pair_of(step)
        cols = pl.ds(pl.multiple_of(pair_n * ND, ND), ND)
        t = dot(blvec[...], att[:, cols], 0, 0)
        for n in range(2):
            pack(1, pair_n * 2 + n, t[:, n * 384 : n * 384 + 384])
        ship_part(2, step)
    for h in (3, 4):
        for step in STEPS:
            ship_part(h, step)
    loss_ref[0] = jnp.sum(loss) / (count.astype(F32) * D)

    def slot_sums(h):
        runs = ((h, 0, 0, 16),) if h != RELAY else ((h, 0, hi * 8, 8), (FAR, 8, hi * 8, 8))

        def one(n, carry):
            rows = pl.ds(pl.multiple_of(n * 16, 16), 16)
            for stream, first, frame, many in runs:
                parts = [got[h, first + f, rows].astype(F32) for f in range(many)]
                for s in range(SC):
                    total = jnp.zeros((16, LANES), F32)
                    for f in range(many):
                        total = total + jnp.where(slot_sm[frame + f] == s, 1.0, 0.0) * parts[f]
                    dense[stream, s, rows] = total
                    dense16[stream, s, rows] = total.astype(BF16)
            return carry

        lax.fori_loop(0, PR[h] // 16, one, 0)
        for stream, *_ in runs:
            for d in (2, 1, 3):
                to = (x + d) % 4
                size = pl.ds(0, SR[stream])
                push(
                    rx_id[stream], dense16.at[stream, pl.ds(to * 4, 4), size],
                    xgot.at[stream, d - 1, :, size], at_x(d),
                )

    def x_sums(h):
        for stream in (h,) if h != RELAY else (h, FAR):
            size = pl.ds(0, SR[stream])
            arrived(rx_id[stream], xgot.at[stream, :, :, size])
            for s in range(4):
                total = dense[stream, pl.ds(x * 4 + s, 1), size][0]
                for d in range(3):
                    total = total + xgot[stream, d, s, size].astype(F32)
                if stream != FAR:
                    xsum[stream, s, size] = total
                xsum16[stream, s, size] = total.astype(BF16)
            if stream == FAR:
                for s in range(4):
                    push(zfar_id, xsum16.at[stream, s, size], zfar.at[zl], across(s))
            else:
                for d in range(1, 4):
                    to = (zl + d) % 4
                    push(
                        rz_id[stream], xsum16.at[stream, to, size], zgot.at[stream, d - 1, size],
                        (x * 4 + to, j),
                    )

    def finish(h):
        size = pl.ds(0, PR[h])
        arrived(rz_id[h], zgot.at[h, :, size])
        total = xsum[h, pl.ds(zl, 1), size][0]
        for d in range(3):
            total = total + zgot[h, d, size].astype(F32)
        if h == RELAY:
            arrived(zfar_id, zfar)
            for d in range(4):
                total = total + zfar[d].astype(F32)
        return total

    def unpack(wide, thin):
        thin = jnp.concatenate([thin, pltpu.roll(thin, 64, 1)], axis=0)
        turned = pltpu.roll(wide, 64, 1)
        lanes = lax.broadcasted_iota(jnp.int32, (64, LANES), 1)
        even = jnp.concatenate([wide, thin], axis=1)
        odd = jnp.concatenate([jnp.where(lanes < 64, thin, turned), turned], axis=1)
        return jnp.where(c == 0, even, odd)[:, :RB]

    def turn(h, *older):
        phase(f"a2a{h}")
        terms_arrived(h)
        phase(f"sums{h}")
        slot_sums(h)
        for g in older:
            phase(f"rsx{g}")
            x_sums(g)

    turn(1)
    turn(0)
    turn(2, 1, 0)
    turn(3)
    turn(4, 2, 3)
    phase("fin01")
    first, second = finish(1), finish(0)
    grad_ref[1] = unpack(jnp.concatenate([first, second[:16]], axis=0), second[16:])
    phase("rsx4")
    x_sums(4)
    phase("fin234")
    first, second, third = finish(2), finish(3), finish(4)
    grad_ref[0] = unpack(
        jnp.concatenate([first, second[:16]], axis=0),
        jnp.concatenate([second[16:], third], axis=0),
    )
    phase("drain")
    for cls in range(2):
        sent(y_id[cls][0][0], like(18))
    sent(x_id[0][0], w.at[pl.ds(0, 21 * HALF), pl.ds(0, 2 * PC)])
    sent(die_id[0], w.at[pl.ds(0, 8 * RB)])
    sent(slot_id, slots.at[pl.ds(0, 15)])
    sent(gx_id, gath.at[pl.ds(0, 3)])
    sent(pick_id, picked.at[pl.ds(0, 15)])
    for h in range(PARTS):
        sent(term_id[h], terms.at[h, pl.ds(0, 14 if h == RELAY else 15), pl.ds(0, PR[h])])
        sent(rz_id[h], zgot.at[h, :, pl.ds(0, PR[h])])
    for stream in range(PARTS + 1):
        sent(rx_id[stream], xgot.at[stream, :, :, pl.ds(0, SR[stream])])
    sent(zfar_id, zfar)
    z_done()
    gz_done()
    phase(None)


def per_device(*args):
    anyspec = pl.BlockSpec(memory_space=pl.ANY)
    vm = pl.BlockSpec(memory_space=pltpu.VMEM)
    sm = pl.BlockSpec(memory_space=pltpu.SMEM)
    big = pltpu.VMEM((FT, D), BF16)
    block = lambda *lead: pltpu.VMEM((*lead, RB, LANES), BF16)
    stream = lambda *lead, dtype=BF16: pltpu.VMEM((PARTS + 1, *lead, PMAX, LANES), dtype)
    part = lambda *lead, dtype=BF16: pltpu.VMEM((PARTS, *lead, PMAX, LANES), dtype)
    grads, loss = pl.pallas_call(
        kernel,
        out_shape=(
            jax.ShapeDtypeStruct((2, RANK, RB), F32),
            jax.ShapeDtypeStruct((1,), F32),
        ),
        in_specs=[anyspec] * 11,
        out_specs=(vm, sm),
        scratch_shapes=[
            pltpu.SMEM((1,), jnp.int32), pltpu.SMEM((SC,), jnp.int32), pltpu.SMEM((1,), jnp.int32),
            pltpu.VMEM((2, RANK, RB), BF16),
            big, big, big, big, big,
            pltpu.VMEM((D, D), BF16),
            big,
            pltpu.VMEM((FT, D), F32),
            big,
            pltpu.VMEM((16, 8, LANES), jnp.int32),
            block(), block(16), block(16), block(16),
            part(16), part(16), stream(16, dtype=F32), stream(16),
            stream(3, 4), part(4, dtype=F32), stream(4), part(3),
            pltpu.VMEM((4, PR[RELAY], LANES), BF16),
            pltpu.VMEM((FT, RANK), BF16),
            pltpu.VMEM((FT, LANES), BF16),
            pltpu.VMEM((FT, RANK), BF16),
            pltpu.SMEM((16,), jnp.int32),
            pltpu.SemaphoreType.DMA((N_SEND,)),
            pltpu.SemaphoreType.DMA((N_RECV,)),
            pltpu.SemaphoreType.DMA((11,)),
        ],
        compiler_params=pltpu.CompilerParams(
            collective_id=0, has_side_effects=True, vmem_limit_bytes=60 * 2**20
        ),
        name="step",
    )(*args)
    return grads[:1], grads[1:], loss


def solution(mesh):
    wide = P(("frame", "fsdp"), None, None)
    flat = P(("frame", "fsdp"))
    adapter = P("frame", None, "fsdp")
    return jax.shard_map(
        per_device,
        mesh=mesh,
        in_specs=(wide,) * 5 + (P("fsdp", None), adapter, adapter, flat, P(), flat),
        out_specs=(adapter, adapter, flat),
        check_vma=False,
    )
```

```python
import functools
import math

import jax
import jax.numpy as jnp
from jax import lax
from jax.experimental import pallas as pl
from jax.experimental.pallas import tpu as pltpu
from jax.sharding import PartitionSpec as P

HEADS = 24
HD = 128
FT = 192
D = 3072
RANK = 64
SC = 16
RB = D // 16
HALF = RB // 2
NB = 512
LANES = 128
K_OWN = 4
K_FAR = 4
PARTS = 5
PR = (48, 48, 48, 32, 16)
PMAX = 48
RELAY = 1
FAR = PARTS
SR = PR + (PR[RELAY],)
MESH = pl.DeviceIdType.MESH
F32 = jnp.float32
BF16 = jnp.bfloat16
SCALE = 1.0 / math.sqrt(HD)


def dot(a, b, ca, cb):
    return lax.dot_general(a, b, (((ca,), (cb,)), ((), ())), preferred_element_type=F32)


class Sems:
    def __init__(self, send, recv):
        self.send, self.recv, self.out, self.into = send, recv, 0, 0

    def sender(self):
        self.out += 1
        return self.out - 1

    def receiver(self):
        self.into += 1
        return self.into - 1

    def copy(self, out, into, src, dst, dev):
        return pltpu.make_async_remote_copy(
            src_ref=src, dst_ref=dst, send_sem=self.send.at[out], recv_sem=self.recv.at[into],
            device_id=dev, device_id_type=MESH,
        )


N_SEND, N_RECV = 36, 68


class Phase:
    def __init__(self):
        self.scope = None

    def __call__(self, name):
        if self.scope is not None:
            self.scope.__exit__(None, None, None)
        self.scope = None
        if name:
            self.scope = jax.named_scope(name)
            self.scope.__enter__()


def kernel(
    q_hbm, k_hbm, v_hbm, res_hbm, tgt_hbm, w_hbm, down_hbm, up_hbm, scene_hbm, row_hbm, count_hbm,
    grad_ref, loss_ref,
    scene_ref, row_ref, count_ref, pair, q, k, v, res, tgt, w, att, acc, cot, slots, bundle, gath, picked, du, terms, got, dense, dense16,
    xgot, xsum, xsum16, zgot, zfar, lvec, lhigh, blvec, slot_sm, ssem, rsem, lsem,
):
    phase = Phase()
    phase("entry")
    sems = Sems(ssem, rsem)
    i = lax.axis_index("frame")
    j = lax.axis_index("fsdp")
    x, zl = i // 4, i % 4
    hi, y, c = j // 8, (j // 2) % 4, j % 2
    far = 1 - hi
    edge = jnp.logical_or(zl == 0, zl == 3)
    inner_zl = jnp.where(zl == 0, 1, 2)

    def fs(h, yy, cc):
        return h * 8 + yy * 2 + cc

    def at_y(dy):
        return (i, fs(hi, (y + dy + 4) % 4, c))

    def at_x(dx):
        return (((x + dx + 4) % 4) * 4 + zl, j)

    partner = (x * 4 + 3 - zl, fs(far, y, c))

    def across(zz):
        return (x * 4 + zz, fs(far, y, c))

    twin = (i, j + 1 - 2 * c)

    barrier = pltpu.get_barrier_semaphore()
    peers = [(i, (j + d) % 16) for d in range(1, 16)]
    peers += [at_x(d) for d in range(1, 4)]
    peers += [(x * 4 + (zl + d) % 4, j) for d in range(1, 4)]
    peers += [across((zl + d) % 4) for d in range(1, 4)]
    for peer in peers:
        pl.semaphore_signal(barrier, inc=1, device_id=peer, device_id_type=MESH)

    pair_loads = [
        pltpu.make_async_copy(src.at[0], pair.at[n], lsem.at[6 + n])
        for n, src in enumerate((down_hbm, up_hbm))
    ]
    pair_loads += [
        pltpu.make_async_copy(src, dst, lsem.at[8 + n])
        for n, (src, dst) in enumerate(
            ((scene_hbm, scene_ref), (row_hbm, row_ref), (count_hbm, count_ref))
        )
    ]
    for cp in pair_loads:
        cp.start()
    loads = []
    for n, (src, dst) in enumerate(((q_hbm, q), (k_hbm, k), (v_hbm, v), (res_hbm, res), (tgt_hbm, tgt))):
        cp = pltpu.make_async_copy(src.at[0], dst, lsem.at[n])
        cp.start()
        loads.append(cp)
    own_row = pl.multiple_of(j * RB, RB)
    own_load = pltpu.make_async_copy(w_hbm, w.at[pl.ds(own_row, RB)], lsem.at[5])
    own_load.start()

    phase("barrier")
    pl.semaphore_wait(barrier, len(peers))

    def quarter(cls, xx):
        kk = K_OWN if cls == 0 else K_FAR
        return pl.ds(pl.multiple_of(xx * (kk * LANES), LANES), kk * LANES)

    def rest(cls, part):
        kk = K_OWN if cls == 0 else K_FAR
        size = (D - 4 * kk * LANES) // 2
        return pl.ds(4 * kk * LANES + part * size, size)

    def shard_row(h, yy):
        return pl.multiple_of(fs(h, yy, c) * RB, RB)

    def half_rows(h, yy, s):
        return pl.ds(pl.multiple_of(shard_row(h, yy) + s * HALF, HALF), HALF)

    def push(ids, src, dst, dev):
        sems.copy(ids[0], ids[1], src, dst, dev).start()

    def arrived(ids, like):
        sems.copy(ids[0], ids[1], like, like, twin).wait_recv()

    def sent(ids, like):
        sems.copy(ids[0], ids[1], like, like, twin).wait_send()

    hs = (hi, far)
    DIRS = (1, -1)
    FIRST = (0, 1)
    PC = K_OWN * LANES

    def like(halves):
        return w.at[pl.ds(0, halves * HALF), pl.ds(0, PC)]

    y_out = [sems.sender() for _ in range(2)]
    y_id = [[[(y_out[cls], sems.receiver()) for _ in range(3)] for _ in range(2)] for cls in range(2)]
    for cls in range(2):
        y_id[cls].append([(y_out[cls], sems.receiver())] + y_id[cls][1][1:])
    z_id = [[(sems.sender(), sems.receiver()) for _ in range(2)] for _ in range(3)]
    shards = [(1, 0), (0, 1), (0, 3), (0, 2), (1, 1), (1, 3), (1, 2)]
    x_out = sems.sender()
    x_id = [[(x_out, sems.receiver()) for _ in range(2)] for _ in range(7)]
    die_out = sems.sender()
    die_id = [(die_out, sems.receiver()) for _ in range(8)]

    def cols_of(cls, piece):
        return quarter(cls, x) if piece == 0 else rest(cls, piece - 1)

    def y_send(cls, piece, from_hbm):
        for n in range(2):
            for dn, d in enumerate(DIRS):
                s = FIRST[dn] if n == 0 else 1 - FIRST[dn]
                cols = cols_of(cls, piece)
                dst = w.at[half_rows(hs[cls], y, s), cols]
                src = w_hbm.at[pl.ds(s * HALF, HALF), cols] if from_hbm else dst
                push(y_id[cls][piece][n], src, dst, at_y(d))

    def y_forward(cls, piece):
        arrived(y_id[cls][piece][0], like(2))
        for dn, d in enumerate(DIRS):
            reg = w.at[half_rows(hs[cls], (y - d + 4) % 4, FIRST[dn]), cols_of(cls, piece)]
            push(y_id[cls][piece][2], reg, reg, at_y(d))

    def y_second(cls, piece):
        arrived(y_id[cls][piece][1], like(4 if piece else 2))

    def y_last(cls, piece):
        arrived(y_id[cls][piece][2], like(4 if piece else 2))

    def x_send(n, s):
        cls, dy = shards[n]
        for dn, d in enumerate(DIRS):
            reg = w.at[half_rows(hs[cls], (y + dy) % 4, s), quarter(cls, x)]
            push(x_id[n][0 if s == FIRST[dn] else 1], reg, reg, at_x(d))

    def x_forward(n):
        cls, dy = shards[n]
        arrived(x_id[n][0], like(2))
        for dn, d in enumerate(DIRS):
            reg = w.at[half_rows(hs[cls], (y + dy) % 4, FIRST[dn]), quarter(cls, (x - d + 4) % 4)]
            push(x_id[n][1], reg, reg, at_x(d))

    def x_finish(n):
        arrived(x_id[n][1], like(4))

    def z_cols(p):
        return cols_of(1, p)

    def z_start():
        @pl.when(edge)
        def _():
            for p in range(3):
                push(z_id[p][0], w_hbm.at[:, z_cols(p)], w.at[pl.ds(own_row, RB), z_cols(p)], partner)

    far_rows = pl.ds(shard_row(far, y), RB)

    def z_edge(p):
        reg = w.at[far_rows, z_cols(p)]

        @pl.when(edge)
        def _():
            arrived(z_id[p][0], reg)
            push(z_id[p][1], reg, reg, (x * 4 + inner_zl, j))

    def z_inner(p):
        reg = w.at[far_rows, z_cols(p)]

        @pl.when(jnp.logical_not(edge))
        def _():
            arrived(z_id[p][1], reg)

    def z_done():
        @pl.when(edge)
        def _():
            for p in range(3):
                reg = w.at[far_rows, z_cols(p)]
                sent(z_id[p][0], reg)
                sent(z_id[p][1], reg)

    mul_order = [(0, 0), (0, 1), (0, 3), (0, 2), (1, 0), (1, 1), (1, 3), (1, 2)]

    def die_send(m, p):
        cls, dy = mul_order[m]
        rows = pl.ds(shard_row(hs[cls], (y + dy) % 4), RB)
        if p == 0:
            cols = [quarter(cls, (x + d) % 4) for d in (1, 3, 2)]
        else:
            cols = [pl.ds(4 * PC, D - 4 * PC) if p == 1 else quarter(cls, x)]
        for at in cols:
            push(die_id[m], w.at[rows, at], w.at[rows, at], twin)

    def die_own():
        rows = pl.ds(own_row, RB)
        push(die_id[0], w_hbm, w.at[rows], twin)

    def die_take(m):
        cls, dy = mul_order[m]
        r = pl.multiple_of(fs(hs[cls], (y + dy) % 4, 1 - c) * RB, RB)
        arrived(die_id[m], w.at[pl.ds(r, RB)])


    def heads(lo, up):
        def one(h, carry):
            cols = pl.ds(pl.multiple_of(h * HD, HD), HD)
            s = dot(q[:, cols], k[:, cols], 1, 1) * SCALE
            pos = lax.broadcasted_iota(jnp.int32, (FT, FT), 1)
            s = jnp.where(pos < count_ref[0], s, -jnp.inf)
            e = jnp.exp(s - jnp.max(s, axis=1, keepdims=True))
            p = (e / jnp.sum(e, axis=1, keepdims=True)).astype(BF16)
            att[:, cols] = dot(p, v[:, cols], 1, 0).astype(BF16)
            return carry

        lax.fori_loop(lo, up, one, 0, unroll=2)

    def rows_of(h):
        return pl.ds(pl.multiple_of(h * (D // 2), D // 2), D // 2)

    def multiply_own():
        def one(n, carry):
            cols = pl.ds(pl.multiple_of(n * NB, NB), NB)
            acc[:, cols] = dot(att[:, rows_of(hi)], w[rows_of(hi), cols], 1, 0)
            return carry

        lax.fori_loop(0, D // NB, one, 0)

    phase("start")
    z_start()
    y_send(0, 0, True)
    for cp in pair_loads:
        cp.wait()
    my_slot = row_ref[scene_ref[0]]
    slots[pl.ds(j, 1)] = jnp.full((1, 8, LANES), my_slot, jnp.int32)
    both = jnp.concatenate([pair[0].astype(F32), pair[1].astype(F32)], axis=0)
    both = jnp.concatenate([both, jnp.zeros((2 * RANK, 256 - RB), F32)], axis=1)
    bundle[...] = both.T[:RB].astype(BF16)
    gath[pl.ds(zl * 4 + x, 1)] = bundle[...][None]

    def gz_copy(dn, t):
        d = DIRS[dn]
        reg = gath.at[pl.ds((zl - d * t) * 4, 4)]
        return sems.copy(*gz_id[dn][t], reg, reg, (x * 4 + zl + d, j))

    def gz_has(dn, t):
        return zl >= t if dn == 0 else zl <= 3 - t

    def gz_goes(dn, t):
        return jnp.logical_and(gz_has(dn, t), zl < 3 if dn == 0 else zl > 0)

    def gz_hop(t):
        for dn in range(2):
            @pl.when(gz_goes(dn, t))
            def _():
                gz_copy(dn, t).start()

    def gz_take(t):
        for dn in range(2):
            @pl.when(gz_has(dn, t + 1))
            def _():
                reg = gath.at[pl.ds((zl - DIRS[dn] * (t + 1)) * 4, 4)]
                arrived(gz_id[dn][t], reg)

    def gz_done():
        for t in range(3):
            for dn in range(2):
                @pl.when(gz_goes(dn, t))
                def _():
                    gz_copy(dn, t).wait_send()

    gz_id = [[(sems.sender(), sems.receiver()) for _ in range(3)] for _ in range(2)]

    def both_ids():
        return sems.sender(), sems.receiver()

    slot_id, gx_id, pick_id, zfar_id = (both_ids() for _ in range(4))
    term_id = [both_ids() for _ in range(PARTS)]
    rx_id = [both_ids() for _ in range(PARTS + 1)]
    rz_id = [both_ids() for _ in range(PARTS)]
    for d in (2, 1, 3):
        push(gx_id, bundle, gath.at[zl * 4 + x], at_x(d))
    for d in range(1, 16):
        push(slot_id, slots.at[j], slots.at[j], (i, (j + d) % 16))

    assert sems.out <= N_SEND and sems.into <= N_RECV
    phase("h0_6")
    for cp in loads[:3]:
        cp.wait()
    heads(0, 6)
    phase("yf00")
    y_forward(0, 0)
    x_send(2, 0)
    x_send(1, 1)
    y_send(0, 1, True)
    y_second(0, 0)
    x_send(2, 1)
    x_send(1, 0)
    phase("ze0")
    die_own()
    die_send(1, 2)
    die_send(2, 2)
    z_edge(0)
    arrived(gx_id, gath.at[pl.ds(0, 3)])
    gz_hop(0)
    phase("h6_12")
    heads(6, 12)
    phase("zi0")
    z_inner(0)
    y_send(1, 0, False)
    x_send(0, 0)
    x_send(0, 1)
    die_send(4, 2)
    y_send(0, 2, True)
    phase("yl00")
    y_last(0, 0)
    x_send(3, 0)
    x_send(3, 1)
    die_send(3, 2)
    phase("yf01")
    y_forward(0, 1)
    phase("ze1")
    z_edge(1)
    gz_take(0)
    gz_hop(1)
    phase("h12_16")
    heads(12, 16)
    phase("xf21")
    x_forward(2)
    x_forward(1)
    phase("yf10")
    y_forward(1, 0)
    x_send(5, 0)
    x_send(4, 1)
    y_second(1, 0)
    x_send(5, 1)
    x_send(4, 0)
    die_send(5, 2)
    die_send(6, 2)
    phase("ze2")
    z_edge(2)
    gz_take(1)
    gz_hop(2)
    phase("h16_20")
    heads(16, 20)
    phase("zi1")
    z_inner(1)
    y_send(1, 1, False)
    phase("xf0")
    x_forward(0)
    phase("h20_24")
    heads(20, 24)
    phase("xf3")
    x_forward(3)
    phase("yf02")
    y_forward(0, 2)
    phase("zi2")
    z_inner(2)
    y_send(1, 2, False)
    phase("slotgz")
    arrived(slot_id, slots.at[pl.ds(0, 15)])
    gz_take(2)
    phase("pick")
    for f in range(16):
        slot_sm[f] = jnp.max(slots[f])
    for f in range(16):
        picked[f] = gath[(slot_sm[f] % 4) * 4 + slot_sm[f] // 4]
    for d in (8, 7, 9, 6, 10, 5, 11, 4, 12, 3, 13, 2, 14, 1, 15):
        to = (j + d) % 16
        push(pick_id, picked.at[to], du.at[j], (i, to))
    du[pl.ds(j, 1)] = picked[pl.ds(j, 1)]
    phase("yl10")
    y_last(1, 0)
    x_send(6, 0)
    x_send(6, 1)
    die_send(7, 2)
    phase("yf11")
    y_forward(1, 1)
    phase("fin12")
    y_second(0, 1)
    die_send(1, 1)
    die_send(2, 1)
    x_finish(2)
    x_finish(1)
    die_send(1, 0)
    die_send(2, 0)
    phase("xf54")
    x_forward(5)
    x_forward(4)
    phase("fin34")
    y_last(0, 1)
    die_send(3, 1)
    die_send(4, 1)
    phase("yf12")
    y_forward(1, 2)
    phase("fin0")
    x_finish(0)
    die_send(4, 0)
    x_finish(3)
    die_send(3, 0)
    phase("xf6")
    x_forward(6)
    phase("ys1")
    y_second(1, 1)
    die_send(5, 1)
    die_send(6, 1)
    phase("mulown")
    own_load.wait()
    for m in range(4):
        die_take(m)
    multiply_own()
    phase("yl1")
    y_last(1, 1)
    die_send(7, 1)
    phase("xfin54")
    x_finish(5)
    die_send(6, 0)
    x_finish(4)
    die_send(5, 0)
    phase("pickwait")
    arrived(pick_id, du.at[pl.ds(0, 15)])
    phase("low")
    lane = lax.broadcasted_iota(jnp.int32, (FT, LANES), 1)

    def low(n, total):
        return total + dot(
            att[:, pl.ds(pl.multiple_of(n * 384, 384), 384)],
            du[pl.ds(n * 2, 2)].reshape(384, LANES), 1, 0,
        )

    lr = lax.fori_loop(0, 8, low, jnp.zeros((FT, LANES), F32), unroll=4).astype(BF16).astype(F32)
    lr = jnp.where(lane < RANK, 2.0 * lr, 0.0)
    lvec[...] = lr[:, :RANK].astype(BF16)
    lhigh[...] = pltpu.roll(lr, RANK, 1).astype(BF16)
    for cp in loads[3:]:
        cp.wait()
    count = count_ref[0]
    row = lax.broadcasted_iota(jnp.int32, (FT, 1), 0)
    valid = row < count
    phase("fin7")
    x_finish(6)
    die_send(7, 0)
    phase("pre")

    def before(n, carry):
        cols = pl.ds(pl.multiple_of(n * 384, 384), 384)
        low_up = dot(lhigh[...], du[pl.ds(n * 2, 2)].reshape(384, LANES), 1, 1)
        acc[:, cols] = acc[:, cols] + low_up + (res[:, cols].astype(F32) - tgt[:, cols].astype(F32))
        return carry

    lax.fori_loop(0, 8, before, 0, unroll=2)
    phase("die456")
    die_take(4)
    die_take(5)
    die_take(6)
    phase("die7")
    die_take(7)
    phase("back")
    inv = 2.0 / count.astype(F32)
    ND = 4 * RB
    chip = j // 2
    half_lane = lax.broadcasted_iota(jnp.int32, (32, LANES), 1) < 64

    def pack(h, n, t):
        top, bottom = t[:32, 128:256], t[32:, 128:256]
        packs = (
            (t[:, :128], jnp.where(half_lane, top, pltpu.roll(bottom, 64, 1))),
            (t[:, 256:], jnp.where(half_lane, pltpu.roll(top, 64, 1), bottom)),
        )
        for b in range(2):
            at = pl.ds(n * 2 + b, 1)
            whole, thin = packs[b]
            whole, thin = whole.astype(BF16)[None], thin.astype(BF16)[None]
            if h == 0:
                terms[1, at] = whole[:, :48]
                terms[0, at, :16] = whole[:, 48:]
                terms[0, at, 16:] = thin
            else:
                terms[2, at] = whole[:, :48]
                terms[3, at, :16] = whole[:, 48:]
                terms[3, at, 16:32] = thin[:, :16]
                terms[4, at, :16] = thin[:, 16:]

    STEPS = (2, 1, 3, 0)

    def pair_of(step):
        return (chip // 2 + step) % 4

    def ship_part(h, step):
        for turn in range(2):
            n = pair_of(step) * 2 + (chip + turn) % 2
            for rel in range(2):
                b = (c + rel) % 2
                block = n * 2 + b
                if h != RELAY:
                    to, at = block, j
                else:
                    to = hi * 8 + (n % 4) * 2 + b
                    at = j % 8 + 8 * far_block(n)
                size = pl.ds(0, PR[h])
                if turn == 0 and rel == 0 and step % (4 if h != RELAY else 2) == 0:
                    got[h, pl.ds(at, 1), size] = terms[h, pl.ds(block, 1), size]
                else:
                    push(term_id[h], terms.at[h, block, size], got.at[h, at, size], (i, to))

    def far_block(n):
        return jnp.where(n // 4 == hi, 0, 1)

    def terms_arrived(h):
        arrived(term_id[h], got.at[h, pl.ds(0, 14 if h == RELAY else 15), pl.ds(0, PR[h])])

    loss = jnp.zeros((8, ND), F32)
    bl = jnp.zeros((FT, LANES), F32)
    for step in STEPS:
        pair_n = pair_of(step)
        cols = pl.ds(pl.multiple_of(pair_n * ND, ND), ND)
        e = acc[:, cols] + dot(att[:, rows_of(far)], w[rows_of(far), cols], 1, 0)
        e = jnp.where(valid, e, 0.0)
        loss = loss + jnp.sum((e * e).reshape(FT // 8, 8, ND), axis=0)
        ct = (inv * e).astype(BF16)
        bl = bl + dot(ct, du[pl.ds(pair_n * 4, 4)].reshape(ND, LANES), 1, 0)
        t = dot(lvec[...], ct, 0, 0)
        for n in range(2):
            pack(0, pair_n * 2 + n, t[:, n * 384 : n * 384 + 384])
        ship_part(1, step)
        ship_part(0, step)
    phase("down")
    blvec[...] = pltpu.roll(2.0 * bl, RANK, 1)[:, :RANK].astype(BF16)
    for step in STEPS:
        pair_n = pair_of(step)
        cols = pl.ds(pl.multiple_of(pair_n * ND, ND), ND)
        t = dot(blvec[...], att[:, cols], 0, 0)
        for n in range(2):
            pack(1, pair_n * 2 + n, t[:, n * 384 : n * 384 + 384])
        ship_part(2, step)
    for h in (3, 4):
        for step in STEPS:
            ship_part(h, step)
    loss_ref[0] = jnp.sum(loss) / (count.astype(F32) * D)

    def slot_sums(h):
        runs = ((h, 0, 0, 16),) if h != RELAY else ((h, 0, hi * 8, 8), (FAR, 8, hi * 8, 8))

        def one(n, carry):
            rows = pl.ds(pl.multiple_of(n * 16, 16), 16)
            for stream, first, frame, many in runs:
                parts = [got[h, first + f, rows].astype(F32) for f in range(many)]
                for s in range(SC):
                    total = jnp.zeros((16, LANES), F32)
                    for f in range(many):
                        total = total + jnp.where(slot_sm[frame + f] == s, 1.0, 0.0) * parts[f]
                    dense[stream, s, rows] = total
                    dense16[stream, s, rows] = total.astype(BF16)
            return carry

        lax.fori_loop(0, PR[h] // 16, one, 0)
        for stream, *_ in runs:
            for d in (2, 1, 3):
                to = (x + d) % 4
                size = pl.ds(0, SR[stream])
                push(
                    rx_id[stream], dense16.at[stream, pl.ds(to * 4, 4), size],
                    xgot.at[stream, d - 1, :, size], at_x(d),
                )

    def x_sums(h):
        for stream in (h,) if h != RELAY else (h, FAR):
            size = pl.ds(0, SR[stream])
            arrived(rx_id[stream], xgot.at[stream, :, :, size])
            for s in range(4):
                total = dense[stream, pl.ds(x * 4 + s, 1), size][0]
                for d in range(3):
                    total = total + xgot[stream, d, s, size].astype(F32)
                if stream != FAR:
                    xsum[stream, s, size] = total
                xsum16[stream, s, size] = total.astype(BF16)
            if stream == FAR:
                for s in range(4):
                    push(zfar_id, xsum16.at[stream, s, size], zfar.at[zl], across(s))
            else:
                for d in range(1, 4):
                    to = (zl + d) % 4
                    push(
                        rz_id[stream], xsum16.at[stream, to, size], zgot.at[stream, d - 1, size],
                        (x * 4 + to, j),
                    )

    def finish(h):
        size = pl.ds(0, PR[h])
        arrived(rz_id[h], zgot.at[h, :, size])
        total = xsum[h, pl.ds(zl, 1), size][0]
        for d in range(3):
            total = total + zgot[h, d, size].astype(F32)
        if h == RELAY:
            arrived(zfar_id, zfar)
            for d in range(4):
                total = total + zfar[d].astype(F32)
        return total

    def unpack(wide, thin):
        thin = jnp.concatenate([thin, pltpu.roll(thin, 64, 1)], axis=0)
        turned = pltpu.roll(wide, 64, 1)
        lanes = lax.broadcasted_iota(jnp.int32, (64, LANES), 1)
        even = jnp.concatenate([wide, thin], axis=1)
        odd = jnp.concatenate([jnp.where(lanes < 64, thin, turned), turned], axis=1)
        return jnp.where(c == 0, even, odd)[:, :RB]

    def turn(h, *older):
        phase(f"a2a{h}")
        terms_arrived(h)
        phase(f"sums{h}")
        slot_sums(h)
        for g in older:
            phase(f"rsx{g}")
            x_sums(g)

    turn(1)
    turn(0)
    turn(2, 1)
    turn(3, 0)
    turn(4, 2, 3)
    phase("fin01")
    first, second = finish(1), finish(0)
    grad_ref[1] = unpack(jnp.concatenate([first, second[:16]], axis=0), second[16:])
    phase("rsx4")
    x_sums(4)
    phase("fin234")
    first, second, third = finish(2), finish(3), finish(4)
    grad_ref[0] = unpack(
        jnp.concatenate([first, second[:16]], axis=0),
        jnp.concatenate([second[16:], third], axis=0),
    )
    phase("drain")
    for cls in range(2):
        sent(y_id[cls][0][0], like(18))
    sent(x_id[0][0], w.at[pl.ds(0, 21 * HALF), pl.ds(0, 2 * PC)])
    sent(die_id[0], w.at[pl.ds(0, 8 * RB)])
    sent(slot_id, slots.at[pl.ds(0, 15)])
    sent(gx_id, gath.at[pl.ds(0, 3)])
    sent(pick_id, picked.at[pl.ds(0, 15)])
    for h in range(PARTS):
        sent(term_id[h], terms.at[h, pl.ds(0, 14 if h == RELAY else 15), pl.ds(0, PR[h])])
        sent(rz_id[h], zgot.at[h, :, pl.ds(0, PR[h])])
    for stream in range(PARTS + 1):
        sent(rx_id[stream], xgot.at[stream, :, :, pl.ds(0, SR[stream])])
    sent(zfar_id, zfar)
    z_done()
    gz_done()
    phase(None)


def per_device(*args):
    anyspec = pl.BlockSpec(memory_space=pl.ANY)
    vm = pl.BlockSpec(memory_space=pltpu.VMEM)
    sm = pl.BlockSpec(memory_space=pltpu.SMEM)
    big = pltpu.VMEM((FT, D), BF16)
    block = lambda *lead: pltpu.VMEM((*lead, RB, LANES), BF16)
    stream = lambda *lead, dtype=BF16: pltpu.VMEM((PARTS + 1, *lead, PMAX, LANES), dtype)
    part = lambda *lead, dtype=BF16: pltpu.VMEM((PARTS, *lead, PMAX, LANES), dtype)
    grads, loss = pl.pallas_call(
        kernel,
        out_shape=(
            jax.ShapeDtypeStruct((2, RANK, RB), F32),
            jax.ShapeDtypeStruct((1,), F32),
        ),
        in_specs=[anyspec] * 11,
        out_specs=(vm, sm),
        scratch_shapes=[
            pltpu.SMEM((1,), jnp.int32), pltpu.SMEM((SC,), jnp.int32), pltpu.SMEM((1,), jnp.int32),
            pltpu.VMEM((2, RANK, RB), BF16),
            big, big, big, big, big,
            pltpu.VMEM((D, D), BF16),
            big,
            pltpu.VMEM((FT, D), F32),
            big,
            pltpu.VMEM((16, 8, LANES), jnp.int32),
            block(), block(16), block(16), block(16),
            part(16), part(16), stream(16, dtype=F32), stream(16),
            stream(3, 4), part(4, dtype=F32), stream(4), part(3),
            pltpu.VMEM((4, PR[RELAY], LANES), BF16),
            pltpu.VMEM((FT, RANK), BF16),
            pltpu.VMEM((FT, LANES), BF16),
            pltpu.VMEM((FT, RANK), BF16),
            pltpu.SMEM((16,), jnp.int32),
            pltpu.SemaphoreType.DMA((N_SEND,)),
            pltpu.SemaphoreType.DMA((N_RECV,)),
            pltpu.SemaphoreType.DMA((11,)),
        ],
        compiler_params=pltpu.CompilerParams(
            collective_id=0, has_side_effects=True, vmem_limit_bytes=60 * 2**20
        ),
        name="step",
    )(*args)
    return grads[:1], grads[1:], loss


def solution(mesh):
    wide = P(("frame", "fsdp"), None, None)
    flat = P(("frame", "fsdp"))
    adapter = P("frame", None, "fsdp")
    return jax.shard_map(
        per_device,
        mesh=mesh,
        in_specs=(wide,) * 5 + (P("fsdp", None), adapter, adapter, flat, P(), flat),
        out_specs=(adapter, adapter, flat),
        check_vma=False,
    )
```
